256 devices in a mesh: section: 8 (over z), shard: 32 (over x, y, core).
Axes of the slice: x: 4, y: 4, z: 8, core: 2. Of those that a mesh axis runs over, the one named last changes fastest.
Arguments:
- deltas: bfloat16 [8, 2, 256, 8192], P('section', None, 'shard'), may hold values from -30 to 30, as said below
- backs: bfloat16 [8, 2, 256, 8192], P('section', None, 'shard'), may hold values from -6 to 6
- gains: float32 [8, 8192], P('section'), may hold values from 0.25 to 1.75
Outputs:
- act_cov: bfloat16 [8, 8192, 8192], P('section', 'shard')
- grad_cov: bfloat16 [8, 8192, 8192], P('section', 'shard')
The draws below stay inside these ranges and needn't reach their ends.
Inputs may be any that keep to these rules, and one draw needn't show every extreme that they name: `deltas`: entries of the section terms, rows and columns of differing scales.
All inputs are finite; a program needn't handle non-finite values.
Results may differ from the reference program's by a relative error of at most 0.0057.
Values may be sent and summed in bfloat16 or wider, within the bound.
A program may use at most 64 MiB of HBM per device.

```python
import math
import jax
import jax.numpy as jnp
from jax import lax

D = 8192
MICRO = 2
TOKENS_MB = 256
TOKENS = 512
SECTIONS = 8


def draw_deltas(key, part):
    first_key = jax.random.fold_in(key, 11)
    second_key = jax.random.fold_in(key, 23)
    third_key = jax.random.fold_in(key, 37)
    full_shape = (SECTIONS, MICRO, TOKENS_MB, D)
    column_scale = jnp.exp(jax.random.uniform(second_key, (D,), jnp.float32, math.log(0.4), math.log(4.0)))
    row_scale = jnp.exp(jax.random.uniform(third_key, (SECTIONS, MICRO, TOKENS_MB, 1), jnp.float32, math.log(0.5), math.log(2.0)))
    base_values = jax.random.normal(first_key, full_shape, jnp.float32)
    return jnp.clip(base_values * column_scale * row_scale, -30.0, 30.0).astype(jnp.bfloat16)


def block_scale(rng, shape, shards, low, largest):
    def one(axis_at, parts):
        heights = jax.random.uniform(jax.random.fold_in(jax.random.fold_in(rng, 6), axis_at), (parts,), jnp.float32, low / len(shards), largest / len(shards))
        return jnp.repeat(jnp.exp(heights), shape[axis_at] // parts).reshape((-1,) + (1,) * (len(shape) - axis_at - 1))

    level = one(*shards[0])
    for cut in shards[1:]:
        level = level * one(*cut)
    return level


def normal_values(own_key, shape, width, most, pieces=(), held_as=jnp.bfloat16):
    result = jax.random.normal(own_key, shape, jnp.float32) * width
    if len(pieces) > 0:
        result = block_scale(own_key, shape, pieces, -0.22, 0.18) * result
    return jnp.clip(result, min=-most, max=most).astype(held_as)


def setup_inputs(seed: int = 0) -> dict:
    key_list = jax.random.split(jax.random.key(seed), 4)
    deltas = draw_deltas(jax.random.fold_in(key_list[3], 71), 0)
    backs = normal_values(key_list[1], (SECTIONS, MICRO, TOKENS_MB, D), 1.0, 6.0, ((0, 8), (2, 32)))
    gains = jnp.clip(1.0 + 0.15 * jax.random.normal(key_list[2], (SECTIONS, D), jnp.float32), 0.25, 1.75)
    return {"deltas": deltas, "backs": backs, "gains": gains}


EPSILON = 1e-05

def reference(deltas, backs, gains):
    forward = jnp.cumsum(deltas.astype(jnp.float32), axis=0)
    backward = jnp.flip(jnp.cumsum(jnp.flip(backs.astype(jnp.float32), 0), axis=0), 0)
    inverse = lax.rsqrt(lax.optimization_barrier(jnp.mean(forward * forward, axis=-1, keepdims=True)) + EPSILON)
    normed = (forward * inverse * gains[:, None, None, :]).astype(jnp.bfloat16)
    grad_bf = backward.astype(jnp.bfloat16)
    model_width = deltas.shape[-1]
    normed = normed.reshape(normed.shape[0], -1, model_width)
    grad_bf = grad_bf.reshape(grad_bf.shape[0], -1, model_width)

    def one_section(section_pair):
        act_rows, grad_rows = section_pair
        act_part = jnp.dot(act_rows.T, act_rows, preferred_element_type=jnp.float32) / TOKENS
        grad_part = jnp.dot(grad_rows.T, grad_rows, preferred_element_type=jnp.float32) / TOKENS
        return (act_part.astype(jnp.bfloat16), grad_part.astype(jnp.bfloat16))
    act_cov, grad_cov = lax.map(one_section, (normed, grad_bf))
    return (act_cov, grad_cov)
```

```python
import functools
import jax
import jax.numpy as jnp
from jax import lax
from jax.experimental import pallas as pl
from jax.experimental.pallas import tpu as pltpu
from jax.sharding import PartitionSpec as P

EPSILON = 1e-05
CHUNKS = 4
RING = 4
PLANE = RING * RING
SENDS = 36
ORDER = (0, 3, 1, 2)


def slot(da, db):
    return da * RING + db


def plane_copies():
    copies = {}
    copies["a+", 0] = (slot(0, 0), slot(3, 0), None, "a+")
    copies["a-", 0] = (slot(0, 0), slot(1, 0), None, "a-")
    copies["a+", 1] = (slot(3, 0), slot(2, 0), 0, "a+")
    copies["a-", 1] = (slot(1, 0), slot(2, 0), 1, "a-")
    for da in ORDER:
        copies["b+", da, 0] = (slot(da, 0), slot(da, 3), None, "b+")
        copies["b-", da, 0] = (slot(da, 0), slot(da, 1), None, "b-")
        copies["b+", da, 1] = (slot(da, 3), slot(da, 2), 0, "b+")
        copies["b-", da, 1] = (slot(da, 1), slot(da, 2), 1, "b-")
    for at in range(PLANE):
        copies["s", at] = (at, PLANE + at, None, "s")
    return copies


def gather_kernel(deltas, backs, gains, g, inp, zbuf, in_sem, zsend, zrecv, send, recv):
    width = inp.shape[-1]
    part = width // CHUNKS
    half_width = width // 2
    sections = lax.axis_size("section")
    s = lax.axis_index("section")
    j = lax.axis_index("shard")
    core = lax.rem(j, 2)
    y = lax.rem(j // 2, RING)
    x = j // (2 * RING)

    def device(px, py, pc):
        return (px * RING + py) * 2 + pc

    xp = device(lax.rem(x + 1, RING), y, core)
    xm = device(lax.rem(x + RING - 1, RING), y, core)
    yp = device(x, lax.rem(y + 1, RING), core)
    ym = device(x, lax.rem(y + RING - 1, RING), core)
    targets = {
        "a+": xp * (1 - core) + yp * core,
        "a-": xm * (1 - core) + ym * core,
        "b+": yp * (1 - core) + xp * core,
        "b-": ym * (1 - core) + xm * core,
        "s": device(x, y, 1 - core),
    }
    copies = plane_copies()
    numbers = {name: at for at, name in enumerate(copies)}

    loads = [
        pltpu.make_async_copy(deltas.at[0], inp.at[0], in_sem.at[0]),
        pltpu.make_async_copy(backs.at[0], inp.at[1], in_sem.at[1]),
    ]
    for load in loads:
        load.start()

    barrier = pltpu.get_barrier_semaphore()
    for target in targets.values():
        pl.semaphore_signal(barrier, device_id=(s, target), device_id_type=pl.DeviceIdType.MESH)
    for step in (1, sections - 1):
        pl.semaphore_signal(
            barrier, device_id=(lax.rem(s + step, sections), j), device_id_type=pl.DeviceIdType.MESH
        )
    pl.semaphore_wait(barrier, len(targets) + 2)
    for load in loads:
        load.wait()

    def copy(t, m, name):
        source, landing, half, target = copies[name]
        at = numbers[name]
        src, dst = g.at[t, m, source], g.at[t, m, landing]
        if half is not None:
            columns = pl.ds(half * half_width, half_width)
            src, dst = src.at[:, columns], dst.at[:, columns]
        return pltpu.make_async_remote_copy(
            src_ref=src,
            dst_ref=dst,
            send_sem=send.at[t, m, at],
            recv_sem=recv.at[t, m, at],
            device_id=(s, targets[target]),
            device_id_type=pl.DeviceIdType.MESH,
        )

    def z_copy(t, m, c):
        return pltpu.make_async_remote_copy(
            src_ref=zbuf.at[t, m, c],
            dst_ref=zbuf.at[t, m, c],
            send_sem=zsend.at[t, m, c],
            recv_sem=zrecv.at[t, m, c],
            device_id=(lax.rem(s + 1 - 2 * t + sections, sections), j),
            device_id_type=pl.DeviceIdType.MESH,
        )

    early = s // (sections // 2)
    middle = ((s == sections // 2) | (s == sections // 2 - 1)).astype(jnp.int32)
    total = 2 * CHUNKS

    def place(t):
        return s * (1 - t) + (sections - 1 - s) * t

    @pl.loop(0, 2 * total)
    def _(e):
        order_apart = e // total
        chunk_apart = lax.rem(e, total)
        lead = 2
        inside = ((e >= lead) & (e < 2 * total - lead)).astype(jnp.int32)
        after = e // (2 * total - lead)
        order_mixed = inside * lax.rem(e, 2) + after
        chunk_mixed = (
            inside * ((1 - lax.rem(e, 2)) * ((e + lead) // 2) + lax.rem(e, 2) * ((e - lead) // 2))
            + after * (e - total)
            + (1 - inside) * (1 - after) * e
        )
        order = middle * order_mixed + (1 - middle) * order_apart
        chunk = middle * chunk_mixed + (1 - middle) * chunk_apart
        t = early + order - 2 * early * order
        m = chunk // CHUNKS
        c = lax.rem(chunk, CHUNKS)
        at = place(t)
        columns = pl.ds(pl.multiple_of(c * part, part), part)

        @pl.when(at > 0)
        def _():
            z_copy(t, m, c).wait_recv()
            zbuf[t, m, c] = zbuf[t, m, c] + inp[t, m, :, columns].astype(jnp.float32)

        @pl.when(at == 0)
        def _():
            zbuf[t, m, c] = inp[t, m, :, columns].astype(jnp.float32)

        @pl.when(at < sections - 1)
        def _():
            z_copy(t, m, c).start()

        @pl.when((c == CHUNKS - 1) & (t == 0))
        def _():
            squares = jnp.zeros((8, 1), jnp.float32)
            for k in range(CHUNKS):
                f = zbuf[0, m, k]
                squares = squares + jnp.sum(f * f, axis=-1, keepdims=True)
            inverse = lax.rsqrt(squares / width + EPSILON)
            for k in range(CHUNKS):
                spot = pl.ds(k * part, part)
                f = zbuf[0, m, k]
                g[0, m, 0, :, spot] = (f * inverse * gains[:, spot]).astype(jnp.bfloat16)

        @pl.when((c == CHUNKS - 1) & (t == 1))
        def _():
            for k in range(CHUNKS):
                g[1, m, 0, :, pl.ds(k * part, part)] = zbuf[1, m, k].astype(jnp.bfloat16)

        @pl.when(c == CHUNKS - 1)
        def _():
            for name in (("a+", 0), ("a-", 0), ("b+", 0, 0), ("b-", 0, 0), ("s", 0)):
                copy(t, m, name).start()

    @pl.loop(0, 4)
    def _(u):
        order = u // 2
        t = early + order - 2 * early * order
        m = lax.rem(u, 2)

        def arrived(*name):
            copy(t, m, name).wait_recv()

        def go(*name):
            copy(t, m, name).start()

        arrived("a+", 0)
        go("a+", 1)
        go("b+", 3, 0)
        go("b-", 3, 0)
        go("s", slot(3, 0))
        arrived("a-", 0)
        go("a-", 1)
        go("b+", 1, 0)
        go("b-", 1, 0)
        go("s", slot(1, 0))
        arrived("b+", 0, 0)
        go("b+", 0, 1)
        go("s", slot(0, 3))
        arrived("b-", 0, 0)
        go("b-", 0, 1)
        go("s", slot(0, 1))
        arrived("a+", 1)
        arrived("a-", 1)
        go("b+", 2, 0)
        go("b-", 2, 0)
        go("s", slot(2, 0))
        for da in (3, 1, 2):
            arrived("b+", da, 0)
            go("b+", da, 1)
            go("s", slot(da, 3))
            arrived("b-", da, 0)
            go("b-", da, 1)
            go("s", slot(da, 1))
        for da in ORDER:
            arrived("b+", da, 1)
            arrived("b-", da, 1)
            go("s", slot(da, 2))

    @pl.loop(0, 4)
    def _(u):
        t = u // 2
        m = lax.rem(u, 2)
        for at in range(PLANE):
            copy(t, m, ("s", at)).wait_recv()
        for name in copies:
            copy(t, m, name).wait_send()

        @pl.when(place(t) < sections - 1)
        def _():
            for c in range(CHUNKS):
                z_copy(t, m, c).wait_send()


def gathered(deltas, backs, gains):
    _, micro, rows, width = deltas.shape
    return pl.pallas_call(
        gather_kernel,
        out_shape=pltpu.VMEM((2, micro, 2 * PLANE, rows, width), jnp.bfloat16),
        in_specs=[
            pl.BlockSpec(memory_space=pl.ANY),
            pl.BlockSpec(memory_space=pl.ANY),
            pl.BlockSpec(memory_space=pltpu.VMEM),
        ],
        out_specs=pl.BlockSpec(memory_space=pltpu.VMEM),
        scratch_shapes=[
            pltpu.VMEM((2, micro, rows, width), jnp.bfloat16),
            pltpu.VMEM((2, micro, CHUNKS, rows, width // CHUNKS), jnp.float32),
            pltpu.SemaphoreType.DMA((2,)),
            pltpu.SemaphoreType.DMA((2, micro, CHUNKS)),
            pltpu.SemaphoreType.DMA((2, micro, CHUNKS)),
            pltpu.SemaphoreType.DMA((2, micro, SENDS)),
            pltpu.SemaphoreType.DMA((2, micro, SENDS)),
        ],
        compiler_params=pltpu.CompilerParams(
            collective_id=0, has_side_effects=True, vmem_limit_bytes=40 * 2**20
        ),
        name="gather",
    )(deltas, backs, gains)


def shards(deltas, backs, gains):
    width = deltas.shape[-1]
    tile_rows = width // lax.axis_size("shard")
    own_start = lax.axis_index("shard") * tile_rows
    g = gathered(deltas, backs, gains)
    tokens = g.shape[1] * g.shape[2] * g.shape[3]
    contract = (((0,), (0,)), ((), ()))
    outs = []
    for t in range(2):
        rows = g[t].reshape(tokens, width)
        left = lax.dynamic_slice_in_dim(rows, own_start, tile_rows, 1)
        full = lax.dot_general(left, rows, contract, preferred_element_type=jnp.float32)
        outs.append((full / tokens).astype(jnp.bfloat16)[None])
    return tuple(outs)


def solution(mesh):
    return jax.shard_map(
        shards,
        mesh=mesh,
        in_specs=(
            P("section", None, "shard", None),
            P("section", None, "shard", None),
            P("section", None),
        ),
        out_specs=(P("section", "shard", None), P("section", "shard", None)),
        check_vma=False,
    )
```

```python
import functools
import jax
import jax.numpy as jnp
from jax import lax
from jax.experimental import pallas as pl
from jax.experimental.pallas import tpu as pltpu
from jax.sharding import PartitionSpec as P

EPSILON = 1e-05
CHUNKS = 4
RING = 4
PLANE = RING * RING
SENDS = 36
ORDER = (0, 3, 1, 2)
BLOCK = 1024


def slot(da, db):
    return da * RING + db


def plane_copies():
    copies = {}
    copies["a+", 0] = (slot(0, 0), slot(3, 0), None, "a+")
    copies["a-", 0] = (slot(0, 0), slot(1, 0), None, "a-")
    copies["a+", 1] = (slot(3, 0), slot(2, 0), 0, "a+")
    copies["a-", 1] = (slot(1, 0), slot(2, 0), 1, "a-")
    for da in ORDER:
        copies["b+", da, 0] = (slot(da, 0), slot(da, 3), None, "b+")
        copies["b-", da, 0] = (slot(da, 0), slot(da, 1), None, "b-")
        copies["b+", da, 1] = (slot(da, 3), slot(da, 2), 0, "b+")
        copies["b-", da, 1] = (slot(da, 1), slot(da, 2), 1, "b-")
    for at in range(PLANE):
        copies["s", at] = (at, PLANE + at, None, "s")
    return copies


def gather_kernel(deltas, backs, gains_in, g, inp, gains, zbuf, in_sem, zsend, zrecv, send, recv):
    width = inp.shape[-1]
    part = width // CHUNKS
    half_width = width // 2
    sections = lax.axis_size("section")
    s = lax.axis_index("section")
    j = lax.axis_index("shard")
    core = lax.rem(j, 2)
    y = lax.rem(j // 2, RING)
    x = j // (2 * RING)

    def device(px, py, pc):
        return (px * RING + py) * 2 + pc

    xp = device(lax.rem(x + 1, RING), y, core)
    xm = device(lax.rem(x + RING - 1, RING), y, core)
    yp = device(x, lax.rem(y + 1, RING), core)
    ym = device(x, lax.rem(y + RING - 1, RING), core)
    targets = {
        "a+": xp * (1 - core) + yp * core,
        "a-": xm * (1 - core) + ym * core,
        "b+": yp * (1 - core) + xp * core,
        "b-": ym * (1 - core) + xm * core,
        "s": device(x, y, 1 - core),
    }
    copies = plane_copies()
    numbers = {name: at for at, name in enumerate(copies)}

    loads = [
        pltpu.make_async_copy(deltas.at[0], inp.at[0], in_sem.at[0]),
        pltpu.make_async_copy(backs.at[0], inp.at[1], in_sem.at[1]),
        pltpu.make_async_copy(gains_in, gains, in_sem.at[2]),
    ]
    for load in loads:
        load.start()

    barrier = pltpu.get_barrier_semaphore()
    for target in targets.values():
        pl.semaphore_signal(barrier, device_id=(s, target), device_id_type=pl.DeviceIdType.MESH)
    for step in (1, sections - 1):
        pl.semaphore_signal(
            barrier, device_id=(lax.rem(s + step, sections), j), device_id_type=pl.DeviceIdType.MESH
        )
    pl.semaphore_wait(barrier, len(targets) + 2)
    for load in loads:
        load.wait()

    def copy(t, m, name):
        source, landing, half, target = copies[name]
        at = numbers[name]
        src, dst = g.at[t, m, source], g.at[t, m, landing]
        if half is not None:
            columns = pl.ds(half * half_width, half_width)
            src, dst = src.at[:, columns], dst.at[:, columns]
        return pltpu.make_async_remote_copy(
            src_ref=src,
            dst_ref=dst,
            send_sem=send.at[t, m, at],
            recv_sem=recv.at[t, m, at],
            device_id=(s, targets[target]),
            device_id_type=pl.DeviceIdType.MESH,
        )

    def z_copy(t, m, c):
        return pltpu.make_async_remote_copy(
            src_ref=zbuf.at[t, m, c],
            dst_ref=zbuf.at[t, m, c],
            send_sem=zsend.at[t, m, c],
            recv_sem=zrecv.at[t, m, c],
            device_id=(lax.rem(s + 1 - 2 * t + sections, sections), j),
            device_id_type=pl.DeviceIdType.MESH,
        )

    early = s // (sections // 2)
    middle = ((s == sections // 2) | (s == sections // 2 - 1)).astype(jnp.int32)
    total = 2 * CHUNKS

    def place(t):
        return s * (1 - t) + (sections - 1 - s) * t

    def z_event(e):
        order_apart = e // total
        chunk_apart = lax.rem(e, total)
        lead = 2
        inside = ((e >= lead) & (e < 2 * total - lead)).astype(jnp.int32)
        after = e // (2 * total - lead)
        order_mixed = inside * lax.rem(e, 2) + after
        chunk_mixed = (
            inside * ((1 - lax.rem(e, 2)) * ((e + lead) // 2) + lax.rem(e, 2) * ((e - lead) // 2))
            + after * (e - total)
            + (1 - inside) * (1 - after) * e
        )
        order = middle * order_mixed + (1 - middle) * order_apart
        chunk = middle * chunk_mixed + (1 - middle) * chunk_apart
        t = early + order - 2 * early * order
        m = chunk // CHUNKS
        c = lax.rem(chunk, CHUNKS)
        at = place(t)
        columns = pl.ds(pl.multiple_of(c * part, part), part)

        @pl.when(at > 0)
        def _():
            z_copy(t, m, c).wait_recv()
            zbuf[t, m, c] = zbuf[t, m, c] + inp[t, m, :, columns].astype(jnp.float32)

        @pl.when(at == 0)
        def _():
            zbuf[t, m, c] = inp[t, m, :, columns].astype(jnp.float32)

        @pl.when(at < sections - 1)
        def _():
            z_copy(t, m, c).start()

        @pl.when((c == CHUNKS - 1) & (t == 0))
        def _():
            squares = jnp.zeros((8, 1), jnp.float32)
            for k in range(CHUNKS):
                f = zbuf[0, m, k]
                squares = squares + jnp.sum(f * f, axis=-1, keepdims=True)
            inverse = lax.rsqrt(squares / width + EPSILON)
            for k in range(CHUNKS):
                spot = pl.ds(k * part, part)
                f = zbuf[0, m, k]
                g[0, m, 0, :, spot] = (f * inverse * gains[:, spot]).astype(jnp.bfloat16)

        @pl.when((c == CHUNKS - 1) & (t == 1))
        def _():
            for k in range(CHUNKS):
                g[1, m, 0, :, pl.ds(k * part, part)] = zbuf[1, m, k].astype(jnp.bfloat16)

        @pl.when(c == CHUNKS - 1)
        def _():
            for name in (("a+", 0), ("a-", 0), ("b+", 0, 0), ("b-", 0, 0), ("s", 0)):
                copy(t, m, name).start()

    def unit(u):
        order = u // 2
        t = early + order - 2 * early * order
        m = lax.rem(u, 2)

        def arrived(*name):
            copy(t, m, name).wait_recv()

        def go(*name):
            copy(t, m, name).start()

        return arrived, go

    def stage_1(u):
        arrived, go = unit(u)
        arrived("a+", 0)
        go("a+", 1)
        go("b+", 3, 0)
        go("b-", 3, 0)
        arrived("a-", 0)
        go("a-", 1)
        go("b+", 1, 0)
        go("b-", 1, 0)
        arrived("b+", 0, 0)
        go("b+", 0, 1)
        arrived("b-", 0, 0)
        go("b-", 0, 1)
        for at in (slot(3, 0), slot(1, 0), slot(0, 3), slot(0, 1)):
            go("s", at)

    def stage_2(u):
        arrived, go = unit(u)
        arrived("a+", 1)
        arrived("a-", 1)
        go("b+", 2, 0)
        go("b-", 2, 0)
        go("s", slot(2, 0))
        for da in (3, 1):
            arrived("b+", da, 0)
            go("b+", da, 1)
            arrived("b-", da, 0)
            go("b-", da, 1)
            go("s", slot(da, 3))
            go("s", slot(da, 1))

    def stage_3(u):
        arrived, go = unit(u)
        arrived("b+", 2, 0)
        go("b+", 2, 1)
        arrived("b-", 2, 0)
        go("b-", 2, 1)
        go("s", slot(2, 3))
        go("s", slot(2, 1))

    def stage_4(u):
        arrived, go = unit(u)
        for da in ORDER:
            arrived("b+", da, 1)
            arrived("b-", da, 1)
            go("s", slot(da, 2))

    stages = (stage_1, stage_2, stage_3, stage_4)
    near = jnp.minimum(s, sections - 1 - s)
    outer = (near == 0).astype(jnp.int32) * 2
    ahead = (
        outer + ((near == 1) | (near == 2)).astype(jnp.int32),
        outer + (near == 1).astype(jnp.int32),
        outer,
        outer,
    )
    split = total * (1 + middle)

    @pl.loop(0, split)
    def _(e):
        z_event(e)

    for stage, count in zip(stages, ahead):

        @pl.loop(0, count)
        def _(u):
            stage(u)

    @pl.loop(split, 2 * total)
    def _(e):
        z_event(e)

    for stage, count in zip(stages, ahead):

        @pl.loop(count, 4)
        def _(u):
            stage(u)

    @pl.loop(0, 4)
    def _(u):
        t = u // 2
        m = lax.rem(u, 2)
        for at in range(PLANE):
            copy(t, m, ("s", at)).wait_recv()
        for name in copies:
            copy(t, m, name).wait_send()

        @pl.when(place(t) < sections - 1)
        def _():
            for c in range(CHUNKS):
                z_copy(t, m, c).wait_send()


def gathered(deltas, backs, gains):
    _, micro, rows, width = deltas.shape
    return pl.pallas_call(
        gather_kernel,
        out_shape=pltpu.VMEM((2, micro, 2 * PLANE, rows, width), jnp.bfloat16),
        in_specs=[
            pl.BlockSpec(memory_space=pl.ANY),
            pl.BlockSpec(memory_space=pl.ANY),
            pl.BlockSpec(memory_space=pl.ANY),
        ],
        out_specs=pl.BlockSpec(memory_space=pltpu.VMEM),
        scratch_shapes=[
            pltpu.VMEM((2, micro, rows, width), jnp.bfloat16),
            pltpu.VMEM((1, width), jnp.float32),
            pltpu.VMEM((2, micro, CHUNKS, rows, width // CHUNKS), jnp.float32),
            pltpu.SemaphoreType.DMA((3,)),
            pltpu.SemaphoreType.DMA((2, micro, CHUNKS)),
            pltpu.SemaphoreType.DMA((2, micro, CHUNKS)),
            pltpu.SemaphoreType.DMA((2, micro, SENDS)),
            pltpu.SemaphoreType.DMA((2, micro, SENDS)),
        ],
        compiler_params=pltpu.CompilerParams(
            collective_id=0, has_side_effects=True, vmem_limit_bytes=40 * 2**20
        ),
        name="gather",
    )(deltas, backs, gains)


def covariance_kernel(g, act, grad, left, rows, sem):
    _, micro, slots, low, width = g.shape
    tokens = micro * slots * low
    tile = left.shape[1]
    steps = width // BLOCK
    start = pl.multiple_of(lax.axis_index("shard") * tile, tile)
    outs = (act, grad)
    for t in range(2):
        own = g[t, :, :, :, pl.ds(start, tile)].reshape(tokens, tile)
        left[t] = own.T

    def block(step):
        return pl.ds(pl.multiple_of(step * BLOCK, BLOCK), BLOCK)

    def write(t, step):
        at = lax.rem(step, 2)
        return pltpu.make_async_copy(rows.at[t, at], outs[t].at[0, :, block(step)], sem.at[t, at])

    @pl.loop(0, steps)
    def _(step):
        for t in range(2):

            @pl.when(step > 1)
            def _():
                write(t, step - 2).wait()

            right = g[t, :, :, :, block(step)].reshape(tokens, BLOCK)
            full = jnp.dot(left[t], right, preferred_element_type=jnp.float32)
            rows[t, lax.rem(step, 2)] = (full / tokens).astype(jnp.bfloat16)
            write(t, step).start()

    for t in range(2):
        for step in (steps - 2, steps - 1):
            write(t, step).wait()


def shards(deltas, backs, gains):
    width = deltas.shape[-1]
    tile = width // lax.axis_size("shard")
    g = gathered(deltas, backs, gains)
    tokens = g.shape[1] * g.shape[2] * g.shape[3]
    out = jax.ShapeDtypeStruct((1, tile, width), jnp.bfloat16)
    return pl.pallas_call(
        covariance_kernel,
        out_shape=(out, out),
        in_specs=[pl.BlockSpec(memory_space=pltpu.VMEM)],
        out_specs=(pl.BlockSpec(memory_space=pl.ANY), pl.BlockSpec(memory_space=pl.ANY)),
        scratch_shapes=[
            pltpu.VMEM((2, tile, tokens), jnp.bfloat16),
            pltpu.VMEM((2, 2, tile, BLOCK), jnp.bfloat16),
            pltpu.SemaphoreType.DMA((2, 2)),
        ],
        compiler_params=pltpu.CompilerParams(vmem_limit_bytes=24 * 2**20),
        name="covariance",
    )(pltpu.with_memory_space_constraint(g, pltpu.VMEM))


def solution(mesh):
    return jax.shard_map(
        shards,
        mesh=mesh,
        in_specs=(
            P("section", None, "shard", None),
            P("section", None, "shard", None),
            P("section", None),
        ),
        out_specs=(P("section", "shard", None), P("section", "shard", None)),
        check_vma=False,
    )
```

```python
import functools
import jax
import jax.numpy as jnp
from jax import lax
from jax.experimental import pallas as pl
from jax.experimental.pallas import tpu as pltpu
from jax.sharding import PartitionSpec as P

EPSILON = 1e-05
CHUNKS = 8
LEAD = 4
RING = 4
PLANE = RING * RING
SENDS = 36
ORDER = (0, 3, 1, 2)
BLOCK = 4096
Z_ENDS = ((16, 16, 21, 22), (16, 19, 31, 31), (16, 22, 31, 31), (30, 32, 31, 31), (32, 32, 32, 32))
STAGE_ENDS = (
    ((1, 1, 1, 1), (2, 1, 1, 2), (2, 2, 1, 2), (2, 2, 1, 2)),
    ((1, 0, 0, 0), (1, 1, 1, 0), (2, 1, 1, 0), (2, 1, 1, 0)),
    ((0, 0, 0, 0), (1, 0, 0, 0), (2, 0, 0, 0), (2, 1, 0, 0)),
    ((0, 0, 0, 0), (0, 0, 0, 0), (0, 0, 0, 0), (1, 0, 0, 0)),
)


GROUPS = (
    ((0, 0), (3, 0), (1, 0), (0, 3), (0, 1), (2, 0), (3, 3), (3, 1)),
    ((1, 3), (1, 1), (2, 3), (2, 1), (0, 2), (3, 2), (1, 2), (2, 2)),
)
GROUP_ENDS = (16, 32)


def slot(da, db):
    start = 0
    for group in GROUPS:
        if (da, db) in group:
            return start + group.index((da, db))
        start += 2 * len(group)


def other(at):
    return at + len(GROUPS[0])


def plane_copies():
    copies = {}
    copies["a+", 0] = (slot(0, 0), slot(3, 0), None, "a+")
    copies["a-", 0] = (slot(0, 0), slot(1, 0), None, "a-")
    copies["a+", 1] = (slot(3, 0), slot(2, 0), 0, "a+")
    copies["a-", 1] = (slot(1, 0), slot(2, 0), 1, "a-")
    for da in ORDER:
        copies["b+", da, 0] = (slot(da, 0), slot(da, 3), None, "b+")
        copies["b-", da, 0] = (slot(da, 0), slot(da, 1), None, "b-")
        copies["b+", da, 1] = (slot(da, 3), slot(da, 2), 0, "b+")
        copies["b-", da, 1] = (slot(da, 1), slot(da, 2), 1, "b-")
    for group in GROUPS:
        for place in group:
            at = slot(*place)
            copies["s", at] = (at, other(at), None, "s")
    return copies


def tokens_of(g, t, group, columns):
    start = GROUP_ENDS[group - 1] if group else 0
    rows = g[t, :, start : GROUP_ENDS[group], :, columns]
    return rows.reshape(rows.shape[0] * rows.shape[1] * rows.shape[2], rows.shape[3])


def own_columns(tile):
    return pl.ds(pl.multiple_of(lax.axis_index("shard") * tile, tile), tile)


def block_columns(step):
    return pl.ds(pl.multiple_of(step * BLOCK, BLOCK), BLOCK)


def gather_kernel(deltas, backs, gains_in, g, part, inp, gains, zbuf, in_sem, zsend, zrecv, send, recv):
    width = inp.shape[-1]
    piece = width // CHUNKS
    half_width = width // 2
    sections = lax.axis_size("section")
    s = lax.axis_index("section")
    j = lax.axis_index("shard")
    core = lax.rem(j, 2)
    y = lax.rem(j // 2, RING)
    x = j // (2 * RING)

    def device(px, py, pc):
        return (px * RING + py) * 2 + pc

    xp = device(lax.rem(x + 1, RING), y, core)
    xm = device(lax.rem(x + RING - 1, RING), y, core)
    yp = device(x, lax.rem(y + 1, RING), core)
    ym = device(x, lax.rem(y + RING - 1, RING), core)
    targets = {
        "a+": xp * (1 - core) + yp * core,
        "a-": xm * (1 - core) + ym * core,
        "b+": yp * (1 - core) + xp * core,
        "b-": ym * (1 - core) + xm * core,
        "s": device(x, y, 1 - core),
    }
    copies = plane_copies()
    numbers = {name: at for at, name in enumerate(copies)}

    loads = [
        pltpu.make_async_copy(deltas.at[0], inp.at[0], in_sem.at[0]),
        pltpu.make_async_copy(backs.at[0], inp.at[1], in_sem.at[1]),
        pltpu.make_async_copy(gains_in, gains, in_sem.at[2]),
    ]
    for load in loads:
        load.start()

    barrier = pltpu.get_barrier_semaphore()
    for target in targets.values():
        pl.semaphore_signal(barrier, device_id=(s, target), device_id_type=pl.DeviceIdType.MESH)
    for step in (1, sections - 1):
        pl.semaphore_signal(
            barrier, device_id=(lax.rem(s + step, sections), j), device_id_type=pl.DeviceIdType.MESH
        )
    pl.semaphore_wait(barrier, len(targets) + 2)
    for load in loads:
        load.wait()

    def copy(t, m, name):
        source, landing, half, target = copies[name]
        at = numbers[name]
        src, dst = g.at[t, m, source], g.at[t, m, landing]
        if half is not None:
            columns = pl.ds(half * half_width, half_width)
            src, dst = src.at[:, columns], dst.at[:, columns]
        return pltpu.make_async_remote_copy(
            src_ref=src,
            dst_ref=dst,
            send_sem=send.at[t, m, at],
            recv_sem=recv.at[t, m, at],
            device_id=(s, targets[target]),
            device_id_type=pl.DeviceIdType.MESH,
        )

    def z_copy(t, m, c):
        return pltpu.make_async_remote_copy(
            src_ref=zbuf.at[t, m, c],
            dst_ref=zbuf.at[t, m, c],
            send_sem=zsend.at[t, m, c],
            recv_sem=zrecv.at[t, m, c],
            device_id=(lax.rem(s + 1 - 2 * t + sections, sections), j),
            device_id_type=pl.DeviceIdType.MESH,
        )

    early = s // (sections // 2)
    middle = ((s == sections // 2) | (s == sections // 2 - 1)).astype(jnp.int32)
    total = 2 * CHUNKS

    def place(t):
        return s * (1 - t) + (sections - 1 - s) * t

    def z_event(e):
        order_apart = e // total
        chunk_apart = lax.rem(e, total)
        lead = LEAD
        inside = ((e >= lead) & (e < 2 * total - lead)).astype(jnp.int32)
        after = e // (2 * total - lead)
        order_mixed = inside * lax.rem(e, 2) + after
        chunk_mixed = (
            inside * ((1 - lax.rem(e, 2)) * ((e + lead) // 2) + lax.rem(e, 2) * ((e - lead) // 2))
            + after * (e - total)
            + (1 - inside) * (1 - after) * e
        )
        order = middle * order_mixed + (1 - middle) * order_apart
        chunk = middle * chunk_mixed + (1 - middle) * chunk_apart
        t = early + order - 2 * early * order
        m = chunk // CHUNKS
        c = lax.rem(chunk, CHUNKS)
        at = place(t)
        columns = pl.ds(pl.multiple_of(c * piece, piece), piece)

        @pl.when(at > 0)
        def _():
            z_copy(t, m, c).wait_recv()
            zbuf[t, m, c] = zbuf[t, m, c] + inp[t, m, :, columns].astype(jnp.float32)

        @pl.when(at == 0)
        def _():
            zbuf[t, m, c] = inp[t, m, :, columns].astype(jnp.float32)

        @pl.when(at < sections - 1)
        def _():
            z_copy(t, m, c).start()

        @pl.when((c == CHUNKS - 1) & (t == 0))
        def _():
            squares = jnp.zeros((8, 1), jnp.float32)
            for k in range(CHUNKS):
                f = zbuf[0, m, k]
                squares = squares + jnp.sum(f * f, axis=-1, keepdims=True)
            inverse = lax.rsqrt(squares / width + EPSILON)
            for k in range(CHUNKS):
                spot = pl.ds(k * piece, piece)
                f = zbuf[0, m, k]
                g[0, m, 0, :, spot] = (f * inverse * gains[:, spot]).astype(jnp.bfloat16)

        @pl.when((c == CHUNKS - 1) & (t == 1))
        def _():
            for k in range(CHUNKS):
                g[1, m, 0, :, pl.ds(k * piece, piece)] = zbuf[1, m, k].astype(jnp.bfloat16)

        @pl.when(c == CHUNKS - 1)
        def _():
            for name in (("a+", 0), ("a-", 0), ("b+", 0, 0), ("b-", 0, 0), ("s", 0)):
                copy(t, m, name).start()

    def unit(u):
        order = u // 2
        t = early + order - 2 * early * order
        m = lax.rem(u, 2)

        def arrived(*name):
            copy(t, m, name).wait_recv()

        def go(*name):
            copy(t, m, name).start()

        return arrived, go

    def stage_1(u):
        arrived, go = unit(u)
        arrived("a+", 0)
        go("a+", 1)
        go("b+", 3, 0)
        go("b-", 3, 0)
        arrived("a-", 0)
        go("a-", 1)
        go("b+", 1, 0)
        go("b-", 1, 0)
        arrived("b+", 0, 0)
        go("b+", 0, 1)
        arrived("b-", 0, 0)
        go("b-", 0, 1)
        for at in (slot(3, 0), slot(1, 0), slot(0, 3), slot(0, 1)):
            go("s", at)

    def stage_2(u):
        arrived, go = unit(u)
        arrived("a+", 1)
        arrived("a-", 1)
        go("b+", 2, 0)
        go("b-", 2, 0)
        go("s", slot(2, 0))
        for da in (3, 1):
            arrived("b+", da, 0)
            go("b+", da, 1)
            arrived("b-", da, 0)
            go("b-", da, 1)
            go("s", slot(da, 3))
            go("s", slot(da, 1))

    def stage_3(u):
        arrived, go = unit(u)
        arrived("b+", 2, 0)
        go("b+", 2, 1)
        arrived("b-", 2, 0)
        go("b-", 2, 1)
        go("s", slot(2, 3))
        go("s", slot(2, 1))

    def stage_4(u):
        arrived, go = unit(u)
        for da in ORDER:
            arrived("b+", da, 1)
            arrived("b-", da, 1)
            go("s", slot(da, 2))

    stages = (stage_1, stage_2, stage_3, stage_4)
    near = jnp.minimum(s, sections - 1 - s)

    def pick(values):
        return sum(value * (near == at).astype(jnp.int32) for at, value in enumerate(values))

    def run(stage, since, ends, permuted=True):
        @pl.loop(pick(since), pick(ends))
        def _(rank):
            swap = (rank == 1).astype(jnp.int32) - (rank == 2).astype(jnp.int32)
            stage(rank + middle * swap if permuted else rank)

    def add_up(order, group):
        t = early + order - 2 * early * order
        for m in range(2):
            for place in GROUPS[group]:
                copy(t, m, ("s", slot(*place))).wait_recv()
        left = tokens_of(g, t, group, own_columns(part.shape[1])).T

        @pl.loop(0, width // BLOCK)
        def _(step):
            columns = block_columns(step)
            more = jnp.dot(
                left, tokens_of(g, t, group, columns), preferred_element_type=jnp.float32
            )
            part[t, :, columns] = part[t, :, columns] + more if group else more

    before = (0, 0, 0, 0)
    for segment, ends in enumerate(Z_ENDS):
        if ends != before:

            @pl.loop(pick(before), pick(ends))
            def _(e):
                z_event(e)

        before = ends
        if segment == len(Z_ENDS) - 1:
            break
        for stage, table in zip(stages, STAGE_ENDS):
            since = table[segment - 1] if segment else (0, 0, 0, 0)
            if table[segment] != since:
                run(stage, since, table[segment])

    since_1, since_2, since_3, since_4 = (table[-1] for table in STAGE_ENDS)
    three, four = (3, 3, 3, 3), (4, 4, 4, 4)
    run(stage_1, since_1, four)
    run(stage_2, since_2, three)
    add_up(0, 0)
    run(stage_2, three, four)
    run(stage_3, since_3, three)
    add_up(1, 0)
    run(stage_3, three, four)

    late = [("s", slot(da, 2)) for da in ORDER]
    rest = [("s", slot(*spot)) for spot in GROUPS[1]]

    @pl.loop(0, 4)
    def _(u):
        t = u // 2
        m = lax.rem(u, 2)
        for name in copies:
            if name not in late:
                copy(t, m, name).wait_send()

        @pl.when(place(t) < sections - 1)
        def _():
            for c in range(CHUNKS):
                z_copy(t, m, c).wait_send()

    run(stage_4, since_4, four, permuted=False)

    @pl.loop(0, 4)
    def _(u):
        t = u // 2
        m = lax.rem(u, 2)
        for name in rest:
            copy(t, m, name).wait_recv()
        for name in late:
            copy(t, m, name).wait_send()


def gathered(deltas, backs, gains):
    _, micro, rows, width = deltas.shape
    return pl.pallas_call(
        gather_kernel,
        out_shape=(
            pltpu.VMEM((2, micro, 2 * PLANE, rows, width), jnp.bfloat16),
            pltpu.VMEM((2, width // lax.axis_size("shard"), width), jnp.float32),
        ),
        in_specs=[
            pl.BlockSpec(memory_space=pltpu.HBM),
            pl.BlockSpec(memory_space=pltpu.HBM),
            pl.BlockSpec(memory_space=pltpu.HBM),
        ],
        out_specs=(pl.BlockSpec(memory_space=pltpu.VMEM), pl.BlockSpec(memory_space=pltpu.VMEM)),
        scratch_shapes=[
            pltpu.VMEM((2, micro, rows, width), jnp.bfloat16),
            pltpu.VMEM((1, width), jnp.float32),
            pltpu.VMEM((2, micro, CHUNKS, rows, width // CHUNKS), jnp.float32),
            pltpu.SemaphoreType.DMA((3,)),
            pltpu.SemaphoreType.DMA((2, micro, CHUNKS)),
            pltpu.SemaphoreType.DMA((2, micro, CHUNKS)),
            pltpu.SemaphoreType.DMA((2, micro, SENDS)),
            pltpu.SemaphoreType.DMA((2, micro, SENDS)),
        ],
        compiler_params=pltpu.CompilerParams(
            collective_id=0, has_side_effects=True, vmem_limit_bytes=20 * 2**20
        ),
        name="gather",
    )(*(pltpu.with_memory_space_constraint(a, pltpu.HBM) for a in (deltas, backs, gains)))


def covariance_kernel(g, part, act, grad, left, rows, sem):
    _, micro, slots, low, width = g.shape
    tokens = micro * slots * low
    tile = part.shape[1]
    steps = width // BLOCK
    last = len(GROUPS) - 1
    outs = (act, grad)
    for t in range(2):
        left[t] = tokens_of(g, t, last, own_columns(tile)).T

    def write(t, step):
        at = lax.rem(step, 2)
        return pltpu.make_async_copy(
            rows.at[t, at], outs[t].at[0, :, block_columns(step)], sem.at[t, at]
        )

    @pl.loop(0, steps)
    def _(step):
        for t in range(2):

            @pl.when(step > 1)
            def _():
                write(t, step - 2).wait()

            columns = block_columns(step)
            right = tokens_of(g, t, last, columns)
            full = part[t, :, columns] + jnp.dot(
                left[t], right, preferred_element_type=jnp.float32
            )
            rows[t, lax.rem(step, 2)] = (full / tokens).astype(jnp.bfloat16)
            write(t, step).start()

    for t in range(2):
        for step in (steps - 2, steps - 1):
            write(t, step).wait()


def shards(deltas, backs, gains):
    width = deltas.shape[-1]
    tile = width // lax.axis_size("shard")
    g, part = gathered(deltas, backs, gains)
    _, micro, slots, low, _ = g.shape
    late_tokens = micro * low * (slots - GROUP_ENDS[-2])
    out = jax.ShapeDtypeStruct((1, tile, width), jnp.bfloat16)
    return pl.pallas_call(
        covariance_kernel,
        out_shape=(out, out),
        in_specs=[pl.BlockSpec(memory_space=pltpu.VMEM)] * 2,
        out_specs=(pl.BlockSpec(memory_space=pl.ANY), pl.BlockSpec(memory_space=pl.ANY)),
        scratch_shapes=[
            pltpu.VMEM((2, tile, late_tokens), jnp.bfloat16),
            pltpu.VMEM((2, 2, tile, BLOCK), jnp.bfloat16),
            pltpu.SemaphoreType.DMA((2, 2)),
        ],
        compiler_params=pltpu.CompilerParams(vmem_limit_bytes=20 * 2**20),
        name="covariance",
    )(*(pltpu.with_memory_space_constraint(a, pltpu.VMEM) for a in (g, part)))


def solution(mesh):
    return jax.shard_map(
        shards,
        mesh=mesh,
        in_specs=(
            P("section", None, "shard", None),
            P("section", None, "shard", None),
            P("section", None),
        ),
        out_specs=(P("section", "shard", None), P("section", "shard", None)),
        check_vma=False,
    )
```

```python
import functools
import jax
import jax.numpy as jnp
from jax import lax
from jax.experimental import pallas as pl
from jax.experimental.pallas import tpu as pltpu
from jax.sharding import PartitionSpec as P

EPSILON = 1e-05
CHUNKS = 8
LEAD = 4
RING = 4
PLANE = RING * RING
ORDER = (0, 3, 1, 2)
BLOCK = 4096
LAST_BLOCK = 2048
LANES = 128
Z_ENDS = (
    (16, 15, 13, 23, 22, 19, 16, 16),
    (16, 16, 22, 24, 22, 29, 19, 16),
    (16, 20, 30, 24, 28, 31, 21, 16),
    (30, 27, 32, 32, 31, 32, 32, 30),
    (32, 32, 32, 32, 32, 32, 32, 32),
)
STAGE_ENDS = (
    (
        (1, 1, 1, 1, 1, 1, 1, 1),
        (2, 1, 1, 1, 1, 1, 1, 2),
        (2, 2, 2, 1, 2, 1, 2, 2),
        (2, 2, 2, 2, 2, 2, 3, 2),
    ),
    (
        (1, 0, 0, 0, 0, 0, 0, 1),
        (1, 1, 1, 0, 0, 1, 1, 1),
        (2, 1, 1, 0, 0, 1, 1, 2),
        (2, 2, 2, 0, 0, 1, 1, 2),
    ),
    (
        (0, 0, 0, 0, 0, 0, 0, 0),
        (1, 0, 0, 0, 0, 0, 0, 1),
        (2, 0, 0, 0, 0, 0, 0, 2),
        (2, 1, 1, 0, 0, 1, 0, 2),
    ),
    (
        (0, 0, 0, 0, 0, 0, 0, 0),
        (0, 0, 0, 0, 0, 0, 0, 0),
        (0, 0, 0, 0, 0, 0, 0, 0),
        (1, 0, 0, 0, 0, 0, 0, 1),
    ),
)


GROUPS = (
    ((0, 0), (3, 0), (1, 0), (0, 3), (0, 1), (2, 0), (3, 3), (3, 1)),
    ((1, 3), (1, 1), (2, 3), (2, 1), (0, 2), (3, 2), (1, 2), (2, 2)),
)
GROUP_ENDS = (16, 32)


def slot(da, db):
    start = 0
    for group in GROUPS:
        if (da, db) in group:
            return start + group.index((da, db))
        start += 2 * len(group)


def other(at):
    return at + len(GROUPS[0])


AXIS, FAR, PAIR, CROSS, CORNER, SIBLING = 0, 1, 2, 6, 7, 8
WAITS = (
    (slot(3, 0), 2),
    (slot(2, 0), 1),
    (slot(0, 3), 2),
    (slot(3, 3), 2),
    (slot(1, 3), 2),
    (slot(2, 3), 2),
    (slot(0, 2), 3),
    (slot(2, 2), 1),
    (other(slot(0, 0)), 8),
    (other(slot(1, 3)), 8),
)


def unit_copies():
    copies = {
        ("a+", 0): (slot(0, 0), slot(3, 0), 1, None, "a+", AXIS),
        ("a-", 0): (slot(0, 0), slot(1, 0), 1, None, "a-", AXIS),
        ("a+", 1): (slot(3, 0), slot(2, 0), 1, 0, "a+", FAR),
        ("a-", 1): (slot(1, 0), slot(2, 0), 1, 1, "a-", FAR),
    }
    for at, da in enumerate(ORDER):
        ahead = CORNER if da == 2 else CROSS
        copies["b+", da, 0] = (slot(da, 0), slot(da, 3), 1, None, "b+", PAIR + at)
        copies["b-", da, 0] = (slot(da, 0), slot(da, 1), 1, None, "b-", PAIR + at)
        copies["b+", da, 1] = (slot(da, 3), slot(da, 2), 1, 0, "b+", ahead)
        copies["b-", da, 1] = (slot(da, 1), slot(da, 2), 1, 1, "b-", ahead)
    for place, count in (
        ((0, 0), 1),
        ((3, 0), 2),
        ((0, 3), 2),
        ((2, 0), 1),
        ((3, 3), 2),
        ((1, 3), 2),
        ((2, 3), 2),
        ((0, 2), 3),
        ((2, 2), 1),
    ):
        at = slot(*place)
        wait = SIBLING + (1 if at >= GROUP_ENDS[0] else 0)
        copies["s", place] = (at, other(at), count, None, "s", wait)
    return copies


def tokens_of(g, t, group, columns):
    start = GROUP_ENDS[group - 1] if group else 0
    rows = g[t, :, start : GROUP_ENDS[group], :, columns]
    return rows.reshape(rows.shape[0] * rows.shape[1] * rows.shape[2], rows.shape[3])


def own_columns(tile):
    return pl.ds(pl.multiple_of(lax.axis_index("shard") * tile, tile), tile)


def block_columns(step):
    return pl.ds(pl.multiple_of(step * BLOCK, BLOCK), BLOCK)


def gather_kernel(deltas, backs, gains_in, g, part, inp, gains, zbuf, squares, in_sem, zsend, zrecv, send, recv):
    width = inp.shape[-1]
    piece = width // CHUNKS
    half_width = width // 2
    sections = lax.axis_size("section")
    s = lax.axis_index("section")
    j = lax.axis_index("shard")
    core = lax.rem(j, 2)
    y = lax.rem(j // 2, RING)
    x = j // (2 * RING)

    def device(px, py, pc):
        return (px * RING + py) * 2 + pc

    xp = device(lax.rem(x + 1, RING), y, core)
    xm = device(lax.rem(x + RING - 1, RING), y, core)
    yp = device(x, lax.rem(y + 1, RING), core)
    ym = device(x, lax.rem(y + RING - 1, RING), core)
    targets = {
        "a+": xp * (1 - core) + yp * core,
        "a-": xm * (1 - core) + ym * core,
        "b+": yp * (1 - core) + xp * core,
        "b-": ym * (1 - core) + xm * core,
        "s": device(x, y, 1 - core),
    }
    copies = unit_copies()

    loads = [
        pltpu.make_async_copy(deltas.at[0], inp.at[0], in_sem.at[0]),
        pltpu.make_async_copy(backs.at[0], inp.at[1], in_sem.at[1]),
        pltpu.make_async_copy(gains_in, gains, in_sem.at[2]),
    ]
    for load in loads:
        load.start()

    barrier = pltpu.get_barrier_semaphore()
    for target in targets.values():
        pl.semaphore_signal(barrier, device_id=(s, target), device_id_type=pl.DeviceIdType.MESH)
    for step in (1, sections - 1):
        pl.semaphore_signal(
            barrier, device_id=(lax.rem(s + step, sections), j), device_id_type=pl.DeviceIdType.MESH
        )
    pl.semaphore_wait(barrier, len(targets) + 2)
    for load in loads:
        load.wait()

    def copy(t, m, name):
        source, landing, count, half, target, wait = copies[name]
        src, dst = g.at[t, m, pl.ds(source, count)], g.at[t, m, pl.ds(landing, count)]
        if half is not None:
            columns = pl.ds(half * half_width, half_width)
            src, dst = src.at[:, :, columns], dst.at[:, :, columns]
        return pltpu.make_async_remote_copy(
            src_ref=src,
            dst_ref=dst,
            send_sem=send.at[t, m],
            recv_sem=recv.at[t, m, wait],
            device_id=(s, targets[target]),
            device_id_type=pl.DeviceIdType.MESH,
        )

    def whole(t, m, start, count, wait):
        places = g.at[t, m, pl.ds(start, count)]
        return pltpu.make_async_remote_copy(
            src_ref=places,
            dst_ref=places,
            send_sem=send.at[t, m],
            recv_sem=recv.at[t, m, wait],
            device_id=(s, targets["s"]),
            device_id_type=pl.DeviceIdType.MESH,
        )

    def take(t, m, wait):
        whole(t, m, *WAITS[wait], wait).wait_recv()

    def z_copy(t, m, c):
        return pltpu.make_async_remote_copy(
            src_ref=zbuf.at[t, m, c],
            dst_ref=zbuf.at[t, m, c],
            send_sem=zsend.at[t],
            recv_sem=zrecv.at[t, m, c],
            device_id=(lax.rem(s + 1 - 2 * t + sections, sections), j),
            device_id_type=pl.DeviceIdType.MESH,
        )

    early = s // (sections // 2)
    middle = ((s == sections // 2) | (s == sections // 2 - 1)).astype(jnp.int32)
    total = 2 * CHUNKS

    def place(t):
        return s * (1 - t) + (sections - 1 - s) * t

    def z_event(e):
        order_apart = e // total
        chunk_apart = lax.rem(e, total)
        lead = LEAD
        inside = ((e >= lead) & (e < 2 * total - lead)).astype(jnp.int32)
        after = e // (2 * total - lead)
        order_mixed = inside * lax.rem(e, 2) + after
        chunk_mixed = (
            inside * ((1 - lax.rem(e, 2)) * ((e + lead) // 2) + lax.rem(e, 2) * ((e - lead) // 2))
            + after * (e - total)
            + (1 - inside) * (1 - after) * e
        )
        order = middle * order_mixed + (1 - middle) * order_apart
        chunk = middle * chunk_mixed + (1 - middle) * chunk_apart
        t = early + order - 2 * early * order
        m = chunk // CHUNKS
        c = lax.rem(chunk, CHUNKS)
        at = place(t)
        columns = pl.ds(pl.multiple_of(c * piece, piece), piece)

        @pl.when(at > 0)
        def _():
            z_copy(t, m, c).wait_recv()
            zbuf[t, m, c] = zbuf[t, m, c] + inp[t, m, :, columns].astype(jnp.float32)

        @pl.when(at == 0)
        def _():
            zbuf[t, m, c] = inp[t, m, :, columns].astype(jnp.float32)

        @pl.when(at < sections - 1)
        def _():
            z_copy(t, m, c).start()

        @pl.when(t == 0)
        def _():
            f = zbuf[0, m, c]
            f = f * f
            more = sum(f[:, k : k + LANES] for k in range(0, piece, LANES))
            squares[m] = jnp.where(c == 0, 0.0, squares[m]) + more

        @pl.when(t == 1)
        def _():
            g[1, m, 0, :, columns] = zbuf[1, m, c].astype(jnp.bfloat16)

        @pl.when((c == CHUNKS - 1) & (t == 0))
        def _():
            total_square = jnp.sum(squares[m], axis=-1, keepdims=True)
            inverse = lax.rsqrt(total_square / width + EPSILON)
            for k in range(CHUNKS):
                spot = pl.ds(k * piece, piece)
                g[0, m, 0, :, spot] = (zbuf[0, m, k] * inverse * gains[:, spot]).astype(
                    jnp.bfloat16
                )

        @pl.when(c == CHUNKS - 1)
        def _():
            for name in (("a+", 0), ("a-", 0), ("b+", 0, 0), ("b-", 0, 0), ("s", (0, 0))):
                copy(t, m, name).start()

    def unit(u):
        order = u // 2
        t = early + order - 2 * early * order
        m = lax.rem(u, 2)

        def arrived(wait):
            take(t, m, wait)

        def go(*names):
            for name in names:
                copy(t, m, name).start()

        return arrived, go

    def stage_1(u):
        arrived, go = unit(u)
        arrived(AXIS)
        go(("a+", 1), ("a-", 1), ("b+", 3, 0), ("b-", 3, 0), ("b+", 1, 0), ("b-", 1, 0))
        go(("s", (3, 0)))
        arrived(PAIR)
        go(("b+", 0, 1), ("b-", 0, 1), ("s", (0, 3)))

    def stage_2(u):
        arrived, go = unit(u)
        arrived(FAR)
        go(("b+", 2, 0), ("b-", 2, 0), ("s", (2, 0)))
        for at, da in enumerate(ORDER):
            if da in (1, 3):
                arrived(PAIR + at)
                go(("b+", da, 1), ("b-", da, 1), ("s", (da, 3)))

    def stage_3(u):
        arrived, go = unit(u)
        arrived(PAIR + ORDER.index(2))
        go(("b+", 2, 1), ("b-", 2, 1), ("s", (2, 3)))

    def stage_4(u):
        arrived, go = unit(u)
        arrived(CROSS)
        go(("s", (0, 2)))
        arrived(CORNER)
        go(("s", (2, 2)))

    stages = (stage_1, stage_2, stage_3, stage_4)
    def pick(values):
        return sum(value * (s == at).astype(jnp.int32) for at, value in enumerate(values))

    none = (0,) * sections

    def run(stage, since, ends, permuted=True):
        @pl.loop(pick(since), pick(ends))
        def _(rank):
            swap = (rank == 1).astype(jnp.int32) - (rank == 2).astype(jnp.int32)
            stage(rank + middle * swap if permuted else rank)

    def add_up(order, group):
        t = early + order - 2 * early * order
        for m in range(2):
            take(t, m, SIBLING + group)
        left = tokens_of(g, t, group, own_columns(part.shape[1])).T

        @pl.loop(0, width // BLOCK)
        def _(step):
            columns = block_columns(step)
            more = jnp.dot(
                left, tokens_of(g, t, group, columns), preferred_element_type=jnp.float32
            )
            part[t, :, columns] = part[t, :, columns] + more if group else more

    before = none
    for segment, ends in enumerate(Z_ENDS):
        if ends != before:

            @pl.loop(pick(before), pick(ends))
            def _(e):
                z_event(e)

        before = ends
        if segment == len(Z_ENDS) - 1:
            break
        for stage, table in zip(stages, STAGE_ENDS):
            since = table[segment - 1] if segment else none
            if table[segment] != since:
                run(stage, since, table[segment])

    since_1, since_2, since_3, since_4 = (table[-1] for table in STAGE_ENDS)
    three, four = (3,) * sections, (4,) * sections
    run(stage_1, since_1, four)
    run(stage_2, since_2, three)
    add_up(0, 0)
    run(stage_2, three, four)
    run(stage_3, since_3, three)
    add_up(1, 0)
    run(stage_3, three, four)

    run(stage_4, since_4, four, permuted=False)

    for t in range(2):
        for m in range(2):
            take(t, m, SIBLING + 1)
            whole(t, m, 0, 2 * PLANE - 1, SIBLING).wait_send()

        @pl.when(place(t) < sections - 1)
        def _():
            pltpu.make_async_remote_copy(
                src_ref=zbuf.at[t],
                dst_ref=zbuf.at[t],
                send_sem=zsend.at[t],
                recv_sem=zrecv.at[t, 0, 0],
                device_id=(lax.rem(s + 1 - 2 * t + sections, sections), j),
                device_id_type=pl.DeviceIdType.MESH,
            ).wait_send()


def gathered(deltas, backs, gains):
    _, micro, rows, width = deltas.shape
    return pl.pallas_call(
        gather_kernel,
        out_shape=(
            pltpu.VMEM((2, micro, 2 * PLANE, rows, width), jnp.bfloat16),
            pltpu.VMEM((2, width // lax.axis_size("shard"), width), jnp.float32),
        ),
        in_specs=[
            pl.BlockSpec(memory_space=pltpu.HBM),
            pl.BlockSpec(memory_space=pltpu.HBM),
            pl.BlockSpec(memory_space=pltpu.HBM),
        ],
        out_specs=(pl.BlockSpec(memory_space=pltpu.VMEM), pl.BlockSpec(memory_space=pltpu.VMEM)),
        scratch_shapes=[
            pltpu.VMEM((2, micro, rows, width), jnp.bfloat16),
            pltpu.VMEM((1, width), jnp.float32),
            pltpu.VMEM((2, micro, CHUNKS, rows, width // CHUNKS), jnp.float32),
            pltpu.VMEM((micro, rows, LANES), jnp.float32),
            pltpu.SemaphoreType.DMA((3,)),
            pltpu.SemaphoreType.DMA((2,)),
            pltpu.SemaphoreType.DMA((2, micro, CHUNKS)),
            pltpu.SemaphoreType.DMA((2, micro)),
            pltpu.SemaphoreType.DMA((2, micro, len(WAITS))),
        ],
        compiler_params=pltpu.CompilerParams(
            collective_id=0, has_side_effects=True, vmem_limit_bytes=20 * 2**20
        ),
        name="gather",
    )(*(pltpu.with_memory_space_constraint(a, pltpu.HBM) for a in (deltas, backs, gains)))


def covariance_kernel(g, part, act, grad, left, rows, sem):
    _, micro, slots, low, width = g.shape
    tokens = micro * slots * low
    tile = part.shape[1]
    last = len(GROUPS) - 1
    outs = (act, grad)
    for t in range(2):
        left[t] = tokens_of(g, t, last, own_columns(tile)).T
    writes = []
    for step in range(width // LAST_BLOCK):
        columns = pl.ds(step * LAST_BLOCK, LAST_BLOCK)
        for t in range(2):
            full = part[t, :, columns] + jnp.dot(
                left[t], tokens_of(g, t, last, columns), preferred_element_type=jnp.float32
            )
            rows[t, :, columns] = (full / tokens).astype(jnp.bfloat16)
            write = pltpu.make_async_copy(
                rows.at[t, :, columns], outs[t].at[0, :, columns], sem.at[t, step]
            )
            write.start()
            writes.append(write)
    for write in writes:
        write.wait()


def shards(deltas, backs, gains):
    width = deltas.shape[-1]
    tile = width // lax.axis_size("shard")
    g, part = gathered(deltas, backs, gains)
    _, micro, slots, low, _ = g.shape
    late_tokens = micro * low * (slots - GROUP_ENDS[-2])
    out = jax.ShapeDtypeStruct((1, tile, width), jnp.bfloat16)
    return pl.pallas_call(
        covariance_kernel,
        out_shape=(out, out),
        in_specs=[pl.BlockSpec(memory_space=pltpu.VMEM)] * 2,
        out_specs=(pl.BlockSpec(memory_space=pl.ANY), pl.BlockSpec(memory_space=pl.ANY)),
        scratch_shapes=[
            pltpu.VMEM((2, tile, late_tokens), jnp.bfloat16),
            pltpu.VMEM((2, tile, width), jnp.bfloat16),
            pltpu.SemaphoreType.DMA((2, width // LAST_BLOCK)),
        ],
        compiler_params=pltpu.CompilerParams(vmem_limit_bytes=20 * 2**20),
        name="covariance",
    )(*(pltpu.with_memory_space_constraint(a, pltpu.VMEM) for a in (g, part)))


def solution(mesh):
    return jax.shard_map(
        shards,
        mesh=mesh,
        in_specs=(
            P("section", None, "shard", None),
            P("section", None, "shard", None),
            P("section", None),
        ),
        out_specs=(P("section", "shard", None), P("section", "shard", None)),
        check_vma=False,
    )
```

```python
import functools
import jax
import jax.numpy as jnp
from jax import lax
from jax.experimental import pallas as pl
from jax.experimental.pallas import tpu as pltpu
from jax.sharding import PartitionSpec as P

EPSILON = 1e-05
CHUNKS = 16
LEADS = (8, 4)
RING = 4
PLANE = RING * RING
ORDER = (0, 3, 1, 2)
BLOCK = 4096
LAST_BLOCK = 2048
LANES = 128
Z_ENDS = (
    (32, 30, 38, 46, 44, 38, 32, 32),
    (32, 32, 58, 48, 44, 58, 38, 32),
    (32, 40, 62, 48, 56, 62, 42, 32),
    (60, 54, 64, 64, 62, 64, 64, 60),
    (64, 64, 64, 64, 64, 64, 64, 64),
)
STAGE_ENDS = (
    (
        (1, 1, 1, 1, 1, 1, 1, 1),
        (2, 1, 1, 1, 1, 1, 1, 2),
        (2, 2, 1, 1, 2, 1, 2, 2),
        (2, 2, 2, 2, 2, 2, 3, 2),
    ),
    (
        (1, 0, 0, 0, 0, 0, 0, 1),
        (1, 1, 1, 0, 0, 1, 1, 1),
        (2, 1, 1, 0, 0, 1, 1, 2),
        (2, 2, 1, 0, 0, 1, 1, 2),
    ),
    (
        (0, 0, 0, 0, 0, 0, 0, 0),
        (1, 0, 0, 0, 0, 0, 0, 1),
        (2, 0, 0, 0, 0, 0, 0, 2),
        (2, 1, 1, 0, 0, 1, 0, 2),
    ),
    (
        (0, 0, 0, 0, 0, 0, 0, 0),
        (0, 0, 0, 0, 0, 0, 0, 0),
        (0, 0, 0, 0, 0, 0, 0, 0),
        (1, 0, 0, 0, 0, 0, 0, 1),
    ),
)


GROUPS = (
    ((0, 0), (3, 0), (1, 0), (0, 3), (0, 1), (2, 0), (3, 3), (3, 1)),
    ((1, 3), (1, 1), (2, 3), (2, 1), (0, 2), (3, 2), (1, 2), (2, 2)),
)
GROUP_ENDS = (16, 32)


def slot(da, db):
    start = 0
    for group in GROUPS:
        if (da, db) in group:
            return start + group.index((da, db))
        start += 2 * len(group)


def other(at):
    return at + len(GROUPS[0])


AXIS, FAR, PAIR, CROSS, CORNER, SIBLING = 0, 1, 2, 6, 7, 8
WAITS = (
    (slot(3, 0), 2),
    (slot(2, 0), 1),
    (slot(0, 3), 2),
    (slot(3, 3), 2),
    (slot(1, 3), 2),
    (slot(2, 3), 2),
    (slot(0, 2), 3),
    (slot(2, 2), 1),
    (other(slot(0, 0)), 8),
    (other(slot(1, 3)), 8),
)


def unit_copies():
    copies = {
        ("a+", 0): (slot(0, 0), slot(3, 0), 1, None, "a+", AXIS),
        ("a-", 0): (slot(0, 0), slot(1, 0), 1, None, "a-", AXIS),
        ("a+", 1): (slot(3, 0), slot(2, 0), 1, 0, "a+", FAR),
        ("a-", 1): (slot(1, 0), slot(2, 0), 1, 1, "a-", FAR),
    }
    for at, da in enumerate(ORDER):
        ahead = CORNER if da == 2 else CROSS
        copies["b+", da, 0] = (slot(da, 0), slot(da, 3), 1, None, "b+", PAIR + at)
        copies["b-", da, 0] = (slot(da, 0), slot(da, 1), 1, None, "b-", PAIR + at)
        copies["b+", da, 1] = (slot(da, 3), slot(da, 2), 1, 0, "b+", ahead)
        copies["b-", da, 1] = (slot(da, 1), slot(da, 2), 1, 1, "b-", ahead)
    for place, count in (
        ((0, 0), 1),
        ((3, 0), 2),
        ((0, 3), 2),
        ((2, 0), 1),
        ((3, 3), 2),
        ((1, 3), 2),
        ((2, 3), 2),
        ((0, 2), 3),
        ((2, 2), 1),
    ):
        at = slot(*place)
        wait = SIBLING + (1 if at >= GROUP_ENDS[0] else 0)
        copies["s", place] = (at, other(at), count, None, "s", wait)
    return copies


def tokens_of(g, t, group, columns):
    start = GROUP_ENDS[group - 1] if group else 0
    rows = g[t, :, start : GROUP_ENDS[group], :, columns]
    return rows.reshape(rows.shape[0] * rows.shape[1] * rows.shape[2], rows.shape[3])


def own_columns(tile):
    return pl.ds(pl.multiple_of(lax.axis_index("shard") * tile, tile), tile)


def block_columns(step):
    return pl.ds(pl.multiple_of(step * BLOCK, BLOCK), BLOCK)


def gather_kernel(deltas, backs, gains_in, g, part, inp, gains, zbuf, squares, in_sem, zsend, zrecv, send, recv):
    width = inp.shape[-1]
    piece = width // CHUNKS
    half_width = width // 2
    sections = lax.axis_size("section")
    s = lax.axis_index("section")
    j = lax.axis_index("shard")
    core = lax.rem(j, 2)
    y = lax.rem(j // 2, RING)
    x = j // (2 * RING)

    def device(px, py, pc):
        return (px * RING + py) * 2 + pc

    xp = device(lax.rem(x + 1, RING), y, core)
    xm = device(lax.rem(x + RING - 1, RING), y, core)
    yp = device(x, lax.rem(y + 1, RING), core)
    ym = device(x, lax.rem(y + RING - 1, RING), core)
    targets = {
        "a+": xp * (1 - core) + yp * core,
        "a-": xm * (1 - core) + ym * core,
        "b+": yp * (1 - core) + xp * core,
        "b-": ym * (1 - core) + xm * core,
        "s": device(x, y, 1 - core),
    }
    copies = unit_copies()

    loads = [
        pltpu.make_async_copy(deltas.at[0], inp.at[0], in_sem.at[0]),
        pltpu.make_async_copy(backs.at[0], inp.at[1], in_sem.at[1]),
        pltpu.make_async_copy(gains_in, gains, in_sem.at[2]),
    ]
    for load in loads:
        load.start()

    barrier = pltpu.get_barrier_semaphore()
    for target in targets.values():
        pl.semaphore_signal(barrier, device_id=(s, target), device_id_type=pl.DeviceIdType.MESH)
    above, below = (s < sections - 1).astype(jnp.int32), (s > 0).astype(jnp.int32)
    for there, step in ((above, 1), (below, -1)):

        @pl.when(there == 1)
        def _():
            pl.semaphore_signal(
                barrier, device_id=(s + step, j), device_id_type=pl.DeviceIdType.MESH
            )

    pl.semaphore_wait(barrier, len(targets) + above + below)
    for load in loads:
        load.wait()

    def copy(t, m, name):
        source, landing, count, half, target, wait = copies[name]
        src, dst = g.at[t, m, pl.ds(source, count)], g.at[t, m, pl.ds(landing, count)]
        if half is not None:
            columns = pl.ds(half * half_width, half_width)
            src, dst = src.at[:, :, columns], dst.at[:, :, columns]
        return pltpu.make_async_remote_copy(
            src_ref=src,
            dst_ref=dst,
            send_sem=send.at[t, m],
            recv_sem=recv.at[t, m, wait],
            device_id=(s, targets[target]),
            device_id_type=pl.DeviceIdType.MESH,
        )

    def whole(t, m, start, count, wait):
        places = g.at[t, m, pl.ds(start, count)]
        return pltpu.make_async_remote_copy(
            src_ref=places,
            dst_ref=places,
            send_sem=send.at[t, m],
            recv_sem=recv.at[t, m, wait],
            device_id=(s, targets["s"]),
            device_id_type=pl.DeviceIdType.MESH,
        )

    def take(t, m, wait):
        whole(t, m, *WAITS[wait], wait).wait_recv()

    def z_copy(t, m, c):
        return pltpu.make_async_remote_copy(
            src_ref=zbuf.at[t, m, c],
            dst_ref=zbuf.at[t, m, c],
            send_sem=zsend.at[t],
            recv_sem=zrecv.at[t, m, c],
            device_id=(lax.rem(s + 1 - 2 * t + sections, sections), j),
            device_id_type=pl.DeviceIdType.MESH,
        )

    early = s // (sections // 2)
    middle = ((s == sections // 2) | (s == sections // 2 - 1)).astype(jnp.int32)
    total = 2 * CHUNKS

    def place(t):
        return s * (1 - t) + (sections - 1 - s) * t

    def z_event(e):
        order_apart = e // total
        chunk_apart = lax.rem(e, total)
        lead = LEADS[0] * (1 - early) + LEADS[1] * early
        inside = ((e >= lead) & (e < 2 * total - lead)).astype(jnp.int32)
        after = (e >= 2 * total - lead).astype(jnp.int32)
        order_mixed = inside * lax.rem(e, 2) + after
        chunk_mixed = (
            inside * ((1 - lax.rem(e, 2)) * ((e + lead) // 2) + lax.rem(e, 2) * ((e - lead) // 2))
            + after * (e - total)
            + (1 - inside) * (1 - after) * e
        )
        order = middle * order_mixed + (1 - middle) * order_apart
        chunk = middle * chunk_mixed + (1 - middle) * chunk_apart
        t = early + order - 2 * early * order
        m = chunk // CHUNKS
        c = lax.rem(chunk, CHUNKS)
        at = place(t)
        columns = pl.ds(pl.multiple_of(c * piece, piece), piece)

        @pl.when(at > 0)
        def _():
            z_copy(t, m, c).wait_recv()
            zbuf[t, m, c] = zbuf[t, m, c] + inp[t, m, :, columns].astype(jnp.float32)

        @pl.when(at == 0)
        def _():
            zbuf[t, m, c] = inp[t, m, :, columns].astype(jnp.float32)

        @pl.when(at < sections - 1)
        def _():
            z_copy(t, m, c).start()

        @pl.when(t == 0)
        def _():
            f = zbuf[0, m, c]
            f = f * f
            more = sum(f[:, k : k + LANES] for k in range(0, piece, LANES))
            squares[m] = jnp.where(c == 0, 0.0, squares[m]) + more

        @pl.when(t == 1)
        def _():
            g[1, m, 0, :, columns] = zbuf[1, m, c].astype(jnp.bfloat16)

        @pl.when((c == CHUNKS - 1) & (t == 0))
        def _():
            total_square = jnp.sum(squares[m], axis=-1, keepdims=True)
            inverse = lax.rsqrt(total_square / width + EPSILON)
            for k in range(CHUNKS):
                spot = pl.ds(k * piece, piece)
                g[0, m, 0, :, spot] = (zbuf[0, m, k] * inverse * gains[:, spot]).astype(
                    jnp.bfloat16
                )

        @pl.when(c == CHUNKS - 1)
        def _():
            for name in (("a+", 0), ("a-", 0), ("b+", 0, 0), ("b-", 0, 0), ("s", (0, 0))):
                copy(t, m, name).start()

    def unit(u):
        order = u // 2
        t = early + order - 2 * early * order
        m = lax.rem(u, 2)

        def arrived(wait):
            take(t, m, wait)

        def go(*names):
            for name in names:
                copy(t, m, name).start()

        return arrived, go

    def stage_1(u):
        arrived, go = unit(u)
        arrived(AXIS)
        go(("a+", 1), ("a-", 1), ("b+", 3, 0), ("b-", 3, 0), ("b+", 1, 0), ("b-", 1, 0))
        go(("s", (3, 0)))
        arrived(PAIR)
        go(("b+", 0, 1), ("b-", 0, 1), ("s", (0, 3)))

    def stage_2(u):
        arrived, go = unit(u)
        arrived(FAR)
        go(("b+", 2, 0), ("b-", 2, 0), ("s", (2, 0)))
        for at, da in enumerate(ORDER):
            if da in (1, 3):
                arrived(PAIR + at)
                go(("b+", da, 1), ("b-", da, 1), ("s", (da, 3)))

    def stage_3(u):
        arrived, go = unit(u)
        arrived(PAIR + ORDER.index(2))
        go(("b+", 2, 1), ("b-", 2, 1), ("s", (2, 3)))

    def stage_4(u):
        arrived, go = unit(u)
        arrived(CROSS)
        go(("s", (0, 2)))
        arrived(CORNER)
        go(("s", (2, 2)))

    stages = (stage_1, stage_2, stage_3, stage_4)
    def pick(values):
        return sum(value * (s == at).astype(jnp.int32) for at, value in enumerate(values))

    none = (0,) * sections

    def run(stage, since, ends, permuted=True):
        @pl.loop(pick(since), pick(ends))
        def _(rank):
            swap = (rank == 1).astype(jnp.int32) - (rank == 2).astype(jnp.int32)
            stage(rank + middle * swap if permuted else rank)

    def add_up(order, group):
        t = early + order - 2 * early * order
        for m in range(2):
            take(t, m, SIBLING + group)
        left = tokens_of(g, t, group, own_columns(part.shape[1])).T

        @pl.loop(0, width // BLOCK)
        def _(step):
            columns = block_columns(step)
            more = jnp.dot(
                left, tokens_of(g, t, group, columns), preferred_element_type=jnp.float32
            )
            part[t, :, columns] = part[t, :, columns] + more if group else more

    before = none
    for segment, ends in enumerate(Z_ENDS):
        if ends != before:

            @pl.loop(pick(before), pick(ends))
            def _(e):
                z_event(e)

        before = ends
        if segment == len(Z_ENDS) - 1:
            break
        for stage, table in zip(stages, STAGE_ENDS):
            since = table[segment - 1] if segment else none
            if table[segment] != since:
                run(stage, since, table[segment])

    since_1, since_2, since_3, since_4 = (table[-1] for table in STAGE_ENDS)
    three, four = (3,) * sections, (4,) * sections
    run(stage_1, since_1, four)
    run(stage_2, since_2, three)
    add_up(0, 0)
    run(stage_2, three, four)
    run(stage_3, since_3, three)
    add_up(1, 0)
    run(stage_3, three, four)

    run(stage_4, since_4, four, permuted=False)

    for t in range(2):
        for m in range(2):
            take(t, m, SIBLING + 1)
            whole(t, m, 0, 2 * PLANE - 1, SIBLING).wait_send()

        @pl.when(place(t) < sections - 1)
        def _():
            pltpu.make_async_remote_copy(
                src_ref=zbuf.at[t],
                dst_ref=zbuf.at[t],
                send_sem=zsend.at[t],
                recv_sem=zrecv.at[t, 0, 0],
                device_id=(lax.rem(s + 1 - 2 * t + sections, sections), j),
                device_id_type=pl.DeviceIdType.MESH,
            ).wait_send()


def gathered(deltas, backs, gains):
    _, micro, rows, width = deltas.shape
    return pl.pallas_call(
        gather_kernel,
        out_shape=(
            pltpu.VMEM((2, micro, 2 * PLANE, rows, width), jnp.bfloat16),
            pltpu.VMEM((2, width // lax.axis_size("shard"), width), jnp.float32),
        ),
        in_specs=[
            pl.BlockSpec(memory_space=pltpu.HBM),
            pl.BlockSpec(memory_space=pltpu.HBM),
            pl.BlockSpec(memory_space=pltpu.HBM),
        ],
        out_specs=(pl.BlockSpec(memory_space=pltpu.VMEM), pl.BlockSpec(memory_space=pltpu.VMEM)),
        scratch_shapes=[
            pltpu.VMEM((2, micro, rows, width), jnp.bfloat16),
            pltpu.VMEM((1, width), jnp.float32),
            pltpu.VMEM((2, micro, CHUNKS, rows, width // CHUNKS), jnp.float32),
            pltpu.VMEM((micro, rows, LANES), jnp.float32),
            pltpu.SemaphoreType.DMA((3,)),
            pltpu.SemaphoreType.DMA((2,)),
            pltpu.SemaphoreType.DMA((2, micro, CHUNKS)),
            pltpu.SemaphoreType.DMA((2, micro)),
            pltpu.SemaphoreType.DMA((2, micro, len(WAITS))),
        ],
        compiler_params=pltpu.CompilerParams(
            collective_id=0, has_side_effects=True, vmem_limit_bytes=20 * 2**20
        ),
        name="gather",
    )(*(pltpu.with_memory_space_constraint(a, pltpu.HBM) for a in (deltas, backs, gains)))


def covariance_kernel(g, part, act, grad, left, rows, sem):
    _, micro, slots, low, width = g.shape
    tokens = micro * slots * low
    tile = part.shape[1]
    last = len(GROUPS) - 1
    outs = (act, grad)
    for t in range(2):
        left[t] = tokens_of(g, t, last, own_columns(tile)).T
    writes = []
    for step in range(width // LAST_BLOCK):
        columns = pl.ds(step * LAST_BLOCK, LAST_BLOCK)
        for t in range(2):
            full = part[t, :, columns] + jnp.dot(
                left[t], tokens_of(g, t, last, columns), preferred_element_type=jnp.float32
            )
            rows[t, :, columns] = (full / tokens).astype(jnp.bfloat16)
            write = pltpu.make_async_copy(
                rows.at[t, :, columns], outs[t].at[0, :, columns], sem.at[t, step]
            )
            write.start()
            writes.append(write)
    for write in writes:
        write.wait()


def shards(deltas, backs, gains):
    width = deltas.shape[-1]
    tile = width // lax.axis_size("shard")
    g, part = gathered(deltas, backs, gains)
    _, micro, slots, low, _ = g.shape
    late_tokens = micro * low * (slots - GROUP_ENDS[-2])
    out = jax.ShapeDtypeStruct((1, tile, width), jnp.bfloat16)
    return pl.pallas_call(
        covariance_kernel,
        out_shape=(out, out),
        in_specs=[pl.BlockSpec(memory_space=pltpu.VMEM)] * 2,
        out_specs=(pl.BlockSpec(memory_space=pl.ANY), pl.BlockSpec(memory_space=pl.ANY)),
        scratch_shapes=[
            pltpu.VMEM((2, tile, late_tokens), jnp.bfloat16),
            pltpu.VMEM((2, tile, width), jnp.bfloat16),
            pltpu.SemaphoreType.DMA((2, width // LAST_BLOCK)),
        ],
        compiler_params=pltpu.CompilerParams(vmem_limit_bytes=20 * 2**20),
        name="covariance",
    )(*(pltpu.with_memory_space_constraint(a, pltpu.VMEM) for a in (g, part)))


def solution(mesh):
    return jax.shard_map(
        shards,
        mesh=mesh,
        in_specs=(
            P("section", None, "shard", None),
            P("section", None, "shard", None),
            P("section", None),
        ),
        out_specs=(P("section", "shard", None), P("section", "shard", None)),
        check_vma=False,
    )
```

```python
import functools
import jax
import jax.numpy as jnp
from jax import lax
from jax.experimental import pallas as pl
from jax.experimental.pallas import tpu as pltpu
from jax.sharding import PartitionSpec as P

EPSILON = 1e-05
CHUNKS = 16
LEADS = (12, 12)
RING = 4
PLANE = RING * RING
ORDER = (0, 3, 1, 2)
BLOCK = 4096
LAST_BLOCK = 2048
LANES = 128
Z_ENDS = (
    (32, 30, 38, 46, 44, 38, 32, 32),
    (32, 32, 58, 48, 44, 58, 38, 32),
    (32, 40, 62, 48, 56, 62, 42, 32),
    (60, 54, 64, 64, 62, 64, 64, 60),
    (64, 64, 64, 64, 64, 64, 64, 64),
)
STAGE_ENDS = (
    (
        (1, 1, 1, 1, 1, 1, 1, 1),
        (2, 1, 1, 1, 1, 1, 1, 2),
        (2, 2, 1, 1, 2, 1, 2, 2),
        (2, 2, 2, 2, 2, 2, 3, 2),
    ),
    (
        (1, 0, 0, 0, 0, 0, 0, 1),
        (1, 1, 1, 0, 0, 1, 1, 1),
        (2, 1, 1, 0, 0, 1, 1, 2),
        (2, 2, 1, 0, 0, 1, 1, 2),
    ),
    (
        (0, 0, 0, 0, 0, 0, 0, 0),
        (1, 0, 0, 0, 0, 0, 0, 1),
        (2, 0, 0, 0, 0, 0, 0, 2),
        (2, 1, 1, 0, 0, 1, 0, 2),
    ),
    (
        (0, 0, 0, 0, 0, 0, 0, 0),
        (0, 0, 0, 0, 0, 0, 0, 0),
        (0, 0, 0, 0, 0, 0, 0, 0),
        (1, 0, 0, 0, 0, 0, 0, 1),
    ),
)


GROUPS = (
    ((0, 0), (3, 0), (1, 0), (0, 3), (0, 1), (2, 0), (3, 3), (3, 1)),
    ((1, 3), (1, 1), (2, 3), (2, 1), (0, 2), (3, 2), (1, 2), (2, 2)),
)
GROUP_ENDS = (16, 32)


def slot(da, db):
    start = 0
    for group in GROUPS:
        if (da, db) in group:
            return start + group.index((da, db))
        start += 2 * len(group)


def other(at):
    return at + len(GROUPS[0])


AXIS, FAR, PAIR, CROSS, CORNER, SIBLING = 0, 1, 2, 6, 7, 8
WAITS = (
    (slot(3, 0), 2),
    (slot(2, 0), 1),
    (slot(0, 3), 2),
    (slot(3, 3), 2),
    (slot(1, 3), 2),
    (slot(2, 3), 2),
    (slot(0, 2), 3),
    (slot(2, 2), 1),
    (other(slot(0, 0)), 8),
    (other(slot(1, 3)), 8),
)


def unit_copies():
    copies = {
        ("a+", 0): (slot(0, 0), slot(3, 0), 1, None, "a+", AXIS),
        ("a-", 0): (slot(0, 0), slot(1, 0), 1, None, "a-", AXIS),
        ("a+", 1): (slot(3, 0), slot(2, 0), 1, 0, "a+", FAR),
        ("a-", 1): (slot(1, 0), slot(2, 0), 1, 1, "a-", FAR),
    }
    for at, da in enumerate(ORDER):
        ahead = CORNER if da == 2 else CROSS
        copies["b+", da, 0] = (slot(da, 0), slot(da, 3), 1, None, "b+", PAIR + at)
        copies["b-", da, 0] = (slot(da, 0), slot(da, 1), 1, None, "b-", PAIR + at)
        copies["b+", da, 1] = (slot(da, 3), slot(da, 2), 1, 0, "b+", ahead)
        copies["b-", da, 1] = (slot(da, 1), slot(da, 2), 1, 1, "b-", ahead)
    for place, count in (
        ((0, 0), 1),
        ((3, 0), 2),
        ((0, 3), 2),
        ((2, 0), 1),
        ((3, 3), 2),
        ((1, 3), 2),
        ((2, 3), 2),
        ((0, 2), 3),
        ((2, 2), 1),
    ):
        at = slot(*place)
        wait = SIBLING + (1 if at >= GROUP_ENDS[0] else 0)
        copies["s", place] = (at, other(at), count, None, "s", wait)
    return copies


def tokens_of(g, t, group, columns):
    start = GROUP_ENDS[group - 1] if group else 0
    rows = g[t, :, start : GROUP_ENDS[group], :, columns]
    return rows.reshape(rows.shape[0] * rows.shape[1] * rows.shape[2], rows.shape[3])


def own_columns(tile):
    return pl.ds(pl.multiple_of(lax.axis_index("shard") * tile, tile), tile)


def block_columns(step):
    return pl.ds(pl.multiple_of(step * BLOCK, BLOCK), BLOCK)


def gather_kernel(deltas, backs, gains_in, g, part, inp, gains, zbuf, squares, in_sem, zsend, zrecv, send, recv):
    width = inp.shape[-1]
    piece = width // CHUNKS
    half_width = width // 2
    sections = lax.axis_size("section")
    s = lax.axis_index("section")
    j = lax.axis_index("shard")
    core = lax.rem(j, 2)
    y = lax.rem(j // 2, RING)
    x = j // (2 * RING)

    def device(px, py, pc):
        return (px * RING + py) * 2 + pc

    xp = device(lax.rem(x + 1, RING), y, core)
    xm = device(lax.rem(x + RING - 1, RING), y, core)
    yp = device(x, lax.rem(y + 1, RING), core)
    ym = device(x, lax.rem(y + RING - 1, RING), core)
    targets = {
        "a+": xp * (1 - core) + yp * core,
        "a-": xm * (1 - core) + ym * core,
        "b+": yp * (1 - core) + xp * core,
        "b-": ym * (1 - core) + xm * core,
        "s": device(x, y, 1 - core),
    }
    copies = unit_copies()

    loads = [
        pltpu.make_async_copy(deltas.at[0], inp.at[0], in_sem.at[0]),
        pltpu.make_async_copy(backs.at[0], inp.at[1], in_sem.at[1]),
        pltpu.make_async_copy(gains_in, gains, in_sem.at[2]),
    ]
    for load in loads:
        load.start()

    barrier = pltpu.get_barrier_semaphore()
    for target in targets.values():
        pl.semaphore_signal(barrier, device_id=(s, target), device_id_type=pl.DeviceIdType.MESH)
    above, below = (s < sections - 1).astype(jnp.int32), (s > 0).astype(jnp.int32)
    for there, step in ((above, 1), (below, -1)):

        @pl.when(there == 1)
        def _():
            pl.semaphore_signal(
                barrier, device_id=(s + step, j), device_id_type=pl.DeviceIdType.MESH
            )

    pl.semaphore_wait(barrier, len(targets) + above + below)
    for load in loads:
        load.wait()

    def copy(t, m, name):
        source, landing, count, half, target, wait = copies[name]
        src, dst = g.at[t, m, pl.ds(source, count)], g.at[t, m, pl.ds(landing, count)]
        if half is not None:
            columns = pl.ds(half * half_width, half_width)
            src, dst = src.at[:, :, columns], dst.at[:, :, columns]
        return pltpu.make_async_remote_copy(
            src_ref=src,
            dst_ref=dst,
            send_sem=send.at[t, m],
            recv_sem=recv.at[t, m, wait],
            device_id=(s, targets[target]),
            device_id_type=pl.DeviceIdType.MESH,
        )

    def whole(t, m, start, count, wait):
        places = g.at[t, m, pl.ds(start, count)]
        return pltpu.make_async_remote_copy(
            src_ref=places,
            dst_ref=places,
            send_sem=send.at[t, m],
            recv_sem=recv.at[t, m, wait],
            device_id=(s, targets["s"]),
            device_id_type=pl.DeviceIdType.MESH,
        )

    def take(t, m, wait):
        whole(t, m, *WAITS[wait], wait).wait_recv()

    def z_copy(t, m, c):
        return pltpu.make_async_remote_copy(
            src_ref=zbuf.at[t, m, c],
            dst_ref=zbuf.at[t, m, c],
            send_sem=zsend.at[t],
            recv_sem=zrecv.at[t, m, c],
            device_id=(lax.rem(s + 1 - 2 * t + sections, sections), j),
            device_id_type=pl.DeviceIdType.MESH,
        )

    early = s // (sections // 2)
    middle = ((s == sections // 2) | (s == sections // 2 - 1)).astype(jnp.int32)
    total = 2 * CHUNKS

    def place(t):
        return s * (1 - t) + (sections - 1 - s) * t

    def z_event(e):
        order_apart = e // total
        chunk_apart = lax.rem(e, total)
        lead = LEADS[0] * (1 - early) + LEADS[1] * early
        inside = ((e >= lead) & (e < 2 * total - lead)).astype(jnp.int32)
        after = (e >= 2 * total - lead).astype(jnp.int32)
        order_mixed = inside * lax.rem(e, 2) + after
        chunk_mixed = (
            inside * ((1 - lax.rem(e, 2)) * ((e + lead) // 2) + lax.rem(e, 2) * ((e - lead) // 2))
            + after * (e - total)
            + (1 - inside) * (1 - after) * e
        )
        order = middle * order_mixed + (1 - middle) * order_apart
        chunk = middle * chunk_mixed + (1 - middle) * chunk_apart
        t = early + order - 2 * early * order
        m = chunk // CHUNKS
        c = lax.rem(chunk, CHUNKS)
        at = place(t)
        columns = pl.ds(pl.multiple_of(c * piece, piece), piece)

        @pl.when(at > 0)
        def _():
            z_copy(t, m, c).wait_recv()
            zbuf[t, m, c] = zbuf[t, m, c] + inp[t, m, :, columns].astype(jnp.float32)

        @pl.when(at == 0)
        def _():
            zbuf[t, m, c] = inp[t, m, :, columns].astype(jnp.float32)

        @pl.when(at < sections - 1)
        def _():
            z_copy(t, m, c).start()

        @pl.when(t == 0)
        def _():
            f = zbuf[0, m, c]
            f = f * f
            more = sum(f[:, k : k + LANES] for k in range(0, piece, LANES))
            squares[m] = jnp.where(c == 0, 0.0, squares[m]) + more

        @pl.when(t == 1)
        def _():
            g[1, m, 0, :, columns] = zbuf[1, m, c].astype(jnp.bfloat16)

        @pl.when((c == CHUNKS - 1) & (t == 0))
        def _():
            total_square = jnp.sum(squares[m], axis=-1, keepdims=True)
            inverse = lax.rsqrt(total_square / width + EPSILON)
            for k in range(CHUNKS):
                spot = pl.ds(k * piece, piece)
                g[0, m, 0, :, spot] = (zbuf[0, m, k] * inverse * gains[:, spot]).astype(
                    jnp.bfloat16
                )

        @pl.when(c == CHUNKS - 1)
        def _():
            for name in (("a+", 0), ("a-", 0), ("b+", 0, 0), ("b-", 0, 0), ("s", (0, 0))):
                copy(t, m, name).start()

    def unit(u):
        order = u // 2
        t = early + order - 2 * early * order
        m = lax.rem(u, 2)

        def arrived(wait):
            take(t, m, wait)

        def go(*names):
            for name in names:
                copy(t, m, name).start()

        return arrived, go

    def stage_1(u):
        arrived, go = unit(u)
        arrived(AXIS)
        go(("a+", 1), ("a-", 1), ("b+", 3, 0), ("b-", 3, 0), ("b+", 1, 0), ("b-", 1, 0))
        go(("s", (3, 0)))
        arrived(PAIR)
        go(("b+", 0, 1), ("b-", 0, 1), ("s", (0, 3)))

    def stage_2(u):
        arrived, go = unit(u)
        arrived(FAR)
        go(("b+", 2, 0), ("b-", 2, 0), ("s", (2, 0)))
        for at, da in enumerate(ORDER):
            if da in (1, 3):
                arrived(PAIR + at)
                go(("b+", da, 1), ("b-", da, 1), ("s", (da, 3)))

    def stage_3(u):
        arrived, go = unit(u)
        arrived(PAIR + ORDER.index(2))
        go(("b+", 2, 1), ("b-", 2, 1), ("s", (2, 3)))

    def stage_4(u):
        arrived, go = unit(u)
        arrived(CROSS)
        go(("s", (0, 2)))
        arrived(CORNER)
        go(("s", (2, 2)))

    stages = (stage_1, stage_2, stage_3, stage_4)
    def pick(values):
        return sum(value * (s == at).astype(jnp.int32) for at, value in enumerate(values))

    none = (0,) * sections

    def run(stage, since, ends, permuted=True):
        @pl.loop(pick(since), pick(ends))
        def _(rank):
            swap = (rank == 1).astype(jnp.int32) - (rank == 2).astype(jnp.int32)
            stage(rank + middle * swap if permuted else rank)

    def add_up(order, group):
        t = early + order - 2 * early * order
        for m in range(2):
            take(t, m, SIBLING + group)
        left = tokens_of(g, t, group, own_columns(part.shape[1])).T

        @pl.loop(0, width // BLOCK)
        def _(step):
            columns = block_columns(step)
            more = jnp.dot(
                left, tokens_of(g, t, group, columns), preferred_element_type=jnp.float32
            )
            part[t, :, columns] = part[t, :, columns] + more if group else more

    before = none
    for segment, ends in enumerate(Z_ENDS):
        if ends != before:

            @pl.loop(pick(before), pick(ends))
            def _(e):
                z_event(e)

        before = ends
        if segment == len(Z_ENDS) - 1:
            break
        for stage, table in zip(stages, STAGE_ENDS):
            since = table[segment - 1] if segment else none
            if table[segment] != since:
                run(stage, since, table[segment])

    since_1, since_2, since_3, since_4 = (table[-1] for table in STAGE_ENDS)
    three, four = (3,) * sections, (4,) * sections
    run(stage_1, since_1, four)
    run(stage_2, since_2, three)
    add_up(0, 0)
    run(stage_2, three, four)
    run(stage_3, since_3, three)
    add_up(1, 0)
    run(stage_3, three, four)

    run(stage_4, since_4, four, permuted=False)

    for t in range(2):
        for m in range(2):
            take(t, m, SIBLING + 1)
            whole(t, m, 0, 2 * PLANE - 1, SIBLING).wait_send()

        @pl.when(place(t) < sections - 1)
        def _():
            pltpu.make_async_remote_copy(
                src_ref=zbuf.at[t],
                dst_ref=zbuf.at[t],
                send_sem=zsend.at[t],
                recv_sem=zrecv.at[t, 0, 0],
                device_id=(lax.rem(s + 1 - 2 * t + sections, sections), j),
                device_id_type=pl.DeviceIdType.MESH,
            ).wait_send()


def gathered(deltas, backs, gains):
    _, micro, rows, width = deltas.shape
    return pl.pallas_call(
        gather_kernel,
        out_shape=(
            pltpu.VMEM((2, micro, 2 * PLANE, rows, width), jnp.bfloat16),
            pltpu.VMEM((2, width // lax.axis_size("shard"), width), jnp.float32),
        ),
        in_specs=[
            pl.BlockSpec(memory_space=pltpu.HBM),
            pl.BlockSpec(memory_space=pltpu.HBM),
            pl.BlockSpec(memory_space=pltpu.HBM),
        ],
        out_specs=(pl.BlockSpec(memory_space=pltpu.VMEM), pl.BlockSpec(memory_space=pltpu.VMEM)),
        scratch_shapes=[
            pltpu.VMEM((2, micro, rows, width), jnp.bfloat16),
            pltpu.VMEM((1, width), jnp.float32),
            pltpu.VMEM((2, micro, CHUNKS, rows, width // CHUNKS), jnp.float32),
            pltpu.VMEM((micro, rows, LANES), jnp.float32),
            pltpu.SemaphoreType.DMA((3,)),
            pltpu.SemaphoreType.DMA((2,)),
            pltpu.SemaphoreType.DMA((2, micro, CHUNKS)),
            pltpu.SemaphoreType.DMA((2, micro)),
            pltpu.SemaphoreType.DMA((2, micro, len(WAITS))),
        ],
        compiler_params=pltpu.CompilerParams(
            collective_id=0, has_side_effects=True, vmem_limit_bytes=20 * 2**20
        ),
        name="gather",
    )(*(pltpu.with_memory_space_constraint(a, pltpu.HBM) for a in (deltas, backs, gains)))


def covariance_kernel(g, part, act, grad, left, rows, sem):
    _, micro, slots, low, width = g.shape
    tokens = micro * slots * low
    tile = part.shape[1]
    last = len(GROUPS) - 1
    outs = (act, grad)
    for t in range(2):
        left[t] = tokens_of(g, t, last, own_columns(tile)).T
    writes = []
    for step in range(width // LAST_BLOCK):
        columns = pl.ds(step * LAST_BLOCK, LAST_BLOCK)
        for t in range(2):
            full = part[t, :, columns] + jnp.dot(
                left[t], tokens_of(g, t, last, columns), preferred_element_type=jnp.float32
            )
            rows[t, :, columns] = (full / tokens).astype(jnp.bfloat16)
            write = pltpu.make_async_copy(
                rows.at[t, :, columns], outs[t].at[0, :, columns], sem.at[t, step]
            )
            write.start()
            writes.append(write)
    for write in writes:
        write.wait()


def shards(deltas, backs, gains):
    width = deltas.shape[-1]
    tile = width // lax.axis_size("shard")
    g, part = gathered(deltas, backs, gains)
    _, micro, slots, low, _ = g.shape
    late_tokens = micro * low * (slots - GROUP_ENDS[-2])
    out = jax.ShapeDtypeStruct((1, tile, width), jnp.bfloat16)
    return pl.pallas_call(
        covariance_kernel,
        out_shape=(out, out),
        in_specs=[pl.BlockSpec(memory_space=pltpu.VMEM)] * 2,
        out_specs=(pl.BlockSpec(memory_space=pl.ANY), pl.BlockSpec(memory_space=pl.ANY)),
        scratch_shapes=[
            pltpu.VMEM((2, tile, late_tokens), jnp.bfloat16),
            pltpu.VMEM((2, tile, width), jnp.bfloat16),
            pltpu.SemaphoreType.DMA((2, width // LAST_BLOCK)),
        ],
        compiler_params=pltpu.CompilerParams(vmem_limit_bytes=20 * 2**20),
        name="covariance",
    )(*(pltpu.with_memory_space_constraint(a, pltpu.VMEM) for a in (g, part)))


def solution(mesh):
    return jax.shard_map(
        shards,
        mesh=mesh,
        in_specs=(
            P("section", None, "shard", None),
            P("section", None, "shard", None),
            P("section", None),
        ),
        out_specs=(P("section", "shard", None), P("section", "shard", None)),
        check_vma=False,
    )
```

```python
import functools
import jax
import jax.numpy as jnp
from jax import lax
from jax.experimental import pallas as pl
from jax.experimental.pallas import tpu as pltpu
from jax.sharding import PartitionSpec as P

EPSILON = 1e-05
CHUNKS = 16
LEADS = (12, 12)
RING = 4
PLANE = RING * RING
ORDER = (0, 3, 1, 2)
BLOCK = 4096
LAST_BLOCK = 1024
LANES = 128
Z_ENDS = (
    (32, 30, 38, 46, 44, 38, 32, 32),
    (32, 32, 58, 48, 44, 58, 38, 32),
    (32, 40, 62, 48, 56, 62, 42, 32),
    (60, 54, 64, 64, 62, 64, 64, 60),
    (64, 64, 64, 64, 64, 64, 64, 64),
)
STAGE_ENDS = (
    (
        (1, 1, 1, 1, 1, 1, 1, 1),
        (2, 1, 1, 1, 1, 1, 1, 2),
        (2, 2, 1, 1, 2, 1, 2, 2),
        (2, 2, 2, 2, 2, 2, 3, 2),
    ),
    (
        (1, 0, 0, 0, 0, 0, 0, 1),
        (1, 1, 1, 0, 0, 1, 1, 1),
        (2, 1, 1, 0, 0, 1, 1, 2),
        (2, 2, 1, 0, 0, 1, 1, 2),
    ),
    (
        (0, 0, 0, 0, 0, 0, 0, 0),
        (1, 0, 0, 0, 0, 0, 0, 1),
        (2, 0, 0, 0, 0, 0, 0, 2),
        (2, 1, 1, 0, 0, 1, 0, 2),
    ),
    (
        (0, 0, 0, 0, 0, 0, 0, 0),
        (0, 0, 0, 0, 0, 0, 0, 0),
        (0, 0, 0, 0, 0, 0, 0, 0),
        (1, 0, 0, 0, 0, 0, 0, 1),
    ),
)


GROUPS = (
    ((0, 0), (3, 0), (1, 0), (0, 3), (0, 1), (2, 0), (3, 3), (3, 1)),
    ((1, 3), (1, 1), (2, 3), (2, 1), (0, 2), (3, 2), (1, 2), (2, 2)),
)
GROUP_ENDS = (16, 32)


def slot(da, db):
    start = 0
    for group in GROUPS:
        if (da, db) in group:
            return start + group.index((da, db))
        start += 2 * len(group)


def other(at):
    return at + len(GROUPS[0])


AXIS, FAR, PAIR, CROSS, CORNER, SIBLING = 0, 1, 2, 6, 7, 8
WAITS = (
    (slot(3, 0), 2),
    (slot(2, 0), 1),
    (slot(0, 3), 2),
    (slot(3, 3), 2),
    (slot(1, 3), 2),
    (slot(2, 3), 2),
    (slot(0, 2), 3),
    (slot(2, 2), 1),
    (other(slot(0, 0)), 8),
    (other(slot(1, 3)), 8),
)


def unit_copies():
    copies = {
        ("a+", 0): (slot(0, 0), slot(3, 0), 1, None, "a+", AXIS),
        ("a-", 0): (slot(0, 0), slot(1, 0), 1, None, "a-", AXIS),
        ("a+", 1): (slot(3, 0), slot(2, 0), 1, 0, "a+", FAR),
        ("a-", 1): (slot(1, 0), slot(2, 0), 1, 1, "a-", FAR),
    }
    for at, da in enumerate(ORDER):
        ahead = CORNER if da == 2 else CROSS
        copies["b+", da, 0] = (slot(da, 0), slot(da, 3), 1, None, "b+", PAIR + at)
        copies["b-", da, 0] = (slot(da, 0), slot(da, 1), 1, None, "b-", PAIR + at)
        copies["b+", da, 1] = (slot(da, 3), slot(da, 2), 1, 0, "b+", ahead)
        copies["b-", da, 1] = (slot(da, 1), slot(da, 2), 1, 1, "b-", ahead)
    for place, count in (
        ((0, 0), 1),
        ((3, 0), 2),
        ((0, 3), 2),
        ((2, 0), 1),
        ((3, 3), 2),
        ((1, 3), 2),
        ((2, 3), 2),
        ((0, 2), 3),
        ((2, 2), 1),
    ):
        at = slot(*place)
        wait = SIBLING + (1 if at >= GROUP_ENDS[0] else 0)
        copies["s", place] = (at, other(at), count, None, "s", wait)
    return copies


def tokens_of(g, t, group, columns):
    start = GROUP_ENDS[group - 1] if group else 0
    rows = g[t, :, start : GROUP_ENDS[group], :, columns]
    return rows.reshape(rows.shape[0] * rows.shape[1] * rows.shape[2], rows.shape[3])


def own_columns(tile):
    return pl.ds(pl.multiple_of(lax.axis_index("shard") * tile, tile), tile)


def block_columns(step):
    return pl.ds(pl.multiple_of(step * BLOCK, BLOCK), BLOCK)


def gather_kernel(deltas, backs, gains_in, g, part, inp, gains, zbuf, squares, in_sem, zsend, zrecv, send, recv):
    width = inp.shape[-1]
    piece = width // CHUNKS
    half_width = width // 2
    sections = lax.axis_size("section")
    s = lax.axis_index("section")
    j = lax.axis_index("shard")
    core = lax.rem(j, 2)
    y = lax.rem(j // 2, RING)
    x = j // (2 * RING)

    def device(px, py, pc):
        return (px * RING + py) * 2 + pc

    xp = device(lax.rem(x + 1, RING), y, core)
    xm = device(lax.rem(x + RING - 1, RING), y, core)
    yp = device(x, lax.rem(y + 1, RING), core)
    ym = device(x, lax.rem(y + RING - 1, RING), core)
    targets = {
        "a+": xp * (1 - core) + yp * core,
        "a-": xm * (1 - core) + ym * core,
        "b+": yp * (1 - core) + xp * core,
        "b-": ym * (1 - core) + xm * core,
        "s": device(x, y, 1 - core),
    }
    copies = unit_copies()

    loads = [
        pltpu.make_async_copy(deltas.at[0], inp.at[0], in_sem.at[0]),
        pltpu.make_async_copy(backs.at[0], inp.at[1], in_sem.at[1]),
        pltpu.make_async_copy(gains_in, gains, in_sem.at[2]),
    ]
    for load in loads:
        load.start()

    barrier = pltpu.get_barrier_semaphore()
    for target in targets.values():
        pl.semaphore_signal(barrier, device_id=(s, target), device_id_type=pl.DeviceIdType.MESH)
    above, below = (s < sections - 1).astype(jnp.int32), (s > 0).astype(jnp.int32)
    for there, step in ((above, 1), (below, -1)):

        @pl.when(there == 1)
        def _():
            pl.semaphore_signal(
                barrier, device_id=(s + step, j), device_id_type=pl.DeviceIdType.MESH
            )

    pl.semaphore_wait(barrier, len(targets) + above + below)
    for load in loads:
        load.wait()

    def copy(t, m, name):
        source, landing, count, half, target, wait = copies[name]
        src, dst = g.at[t, m, pl.ds(source, count)], g.at[t, m, pl.ds(landing, count)]
        if half is not None:
            columns = pl.ds(half * half_width, half_width)
            src, dst = src.at[:, :, columns], dst.at[:, :, columns]
        return pltpu.make_async_remote_copy(
            src_ref=src,
            dst_ref=dst,
            send_sem=send.at[t, m],
            recv_sem=recv.at[t, m, wait],
            device_id=(s, targets[target]),
            device_id_type=pl.DeviceIdType.MESH,
        )

    def whole(t, m, start, count, wait):
        places = g.at[t, m, pl.ds(start, count)]
        return pltpu.make_async_remote_copy(
            src_ref=places,
            dst_ref=places,
            send_sem=send.at[t, m],
            recv_sem=recv.at[t, m, wait],
            device_id=(s, targets["s"]),
            device_id_type=pl.DeviceIdType.MESH,
        )

    def take(t, m, wait):
        whole(t, m, *WAITS[wait], wait).wait_recv()

    def z_copy(t, m, c):
        return pltpu.make_async_remote_copy(
            src_ref=zbuf.at[t, m, c],
            dst_ref=zbuf.at[t, m, c],
            send_sem=zsend.at[t],
            recv_sem=zrecv.at[t, m, c],
            device_id=(lax.rem(s + 1 - 2 * t + sections, sections), j),
            device_id_type=pl.DeviceIdType.MESH,
        )

    early = s // (sections // 2)
    middle = ((s == sections // 2) | (s == sections // 2 - 1)).astype(jnp.int32)
    total = 2 * CHUNKS

    def place(t):
        return s * (1 - t) + (sections - 1 - s) * t

    def z_event(e):
        order_apart = e // total
        chunk_apart = lax.rem(e, total)
        lead = LEADS[0] * (1 - early) + LEADS[1] * early
        inside = ((e >= lead) & (e < 2 * total - lead)).astype(jnp.int32)
        after = (e >= 2 * total - lead).astype(jnp.int32)
        order_mixed = inside * lax.rem(e, 2) + after
        chunk_mixed = (
            inside * ((1 - lax.rem(e, 2)) * ((e + lead) // 2) + lax.rem(e, 2) * ((e - lead) // 2))
            + after * (e - total)
            + (1 - inside) * (1 - after) * e
        )
        order = middle * order_mixed + (1 - middle) * order_apart
        chunk = middle * chunk_mixed + (1 - middle) * chunk_apart
        t = early + order - 2 * early * order
        m = chunk // CHUNKS
        c = lax.rem(chunk, CHUNKS)
        at = place(t)
        columns = pl.ds(pl.multiple_of(c * piece, piece), piece)

        @pl.when(at > 0)
        def _():
            z_copy(t, m, c).wait_recv()
            zbuf[t, m, c] = zbuf[t, m, c] + inp[t, m, :, columns].astype(jnp.float32)

        @pl.when(at == 0)
        def _():
            zbuf[t, m, c] = inp[t, m, :, columns].astype(jnp.float32)

        @pl.when(at < sections - 1)
        def _():
            z_copy(t, m, c).start()

        @pl.when(t == 0)
        def _():
            f = zbuf[0, m, c]
            f = f * f
            more = sum(f[:, k : k + LANES] for k in range(0, piece, LANES))
            squares[m] = jnp.where(c == 0, 0.0, squares[m]) + more

        @pl.when(t == 1)
        def _():
            g[1, m, 0, :, columns] = zbuf[1, m, c].astype(jnp.bfloat16)

        @pl.when((c == CHUNKS - 1) & (t == 0))
        def _():
            total_square = jnp.sum(squares[m], axis=-1, keepdims=True)
            inverse = lax.rsqrt(total_square / width + EPSILON)
            for k in range(CHUNKS):
                spot = pl.ds(k * piece, piece)
                g[0, m, 0, :, spot] = (zbuf[0, m, k] * inverse * gains[:, spot]).astype(
                    jnp.bfloat16
                )

        @pl.when(c == CHUNKS - 1)
        def _():
            for name in (("a+", 0), ("a-", 0), ("b+", 0, 0), ("b-", 0, 0), ("s", (0, 0))):
                copy(t, m, name).start()

    def unit(u):
        order = u // 2
        t = early + order - 2 * early * order
        m = lax.rem(u, 2)

        def arrived(wait):
            take(t, m, wait)

        def go(*names):
            for name in names:
                copy(t, m, name).start()

        return arrived, go

    def stage_1(u):
        arrived, go = unit(u)
        arrived(AXIS)
        go(("a+", 1), ("a-", 1), ("b+", 3, 0), ("b-", 3, 0), ("b+", 1, 0), ("b-", 1, 0))
        go(("s", (3, 0)))
        arrived(PAIR)
        go(("b+", 0, 1), ("b-", 0, 1), ("s", (0, 3)))

    def stage_2(u):
        arrived, go = unit(u)
        arrived(FAR)
        go(("b+", 2, 0), ("b-", 2, 0), ("s", (2, 0)))
        for at, da in enumerate(ORDER):
            if da in (1, 3):
                arrived(PAIR + at)
                go(("b+", da, 1), ("b-", da, 1), ("s", (da, 3)))

    def stage_3(u):
        arrived, go = unit(u)
        arrived(PAIR + ORDER.index(2))
        go(("b+", 2, 1), ("b-", 2, 1), ("s", (2, 3)))

    def stage_4(u):
        arrived, go = unit(u)
        arrived(CROSS)
        go(("s", (0, 2)))
        arrived(CORNER)
        go(("s", (2, 2)))

    stages = (stage_1, stage_2, stage_3, stage_4)
    def pick(values):
        return sum(value * (s == at).astype(jnp.int32) for at, value in enumerate(values))

    none = (0,) * sections

    def run(stage, since, ends, permuted=True):
        @pl.loop(pick(since), pick(ends))
        def _(rank):
            swap = (rank == 1).astype(jnp.int32) - (rank == 2).astype(jnp.int32)
            stage(rank + middle * swap if permuted else rank)

    def add_up(order, group):
        t = early + order - 2 * early * order
        for m in range(2):
            take(t, m, SIBLING + group)
        left = tokens_of(g, t, group, own_columns(part.shape[1])).T

        @pl.loop(0, width // BLOCK)
        def _(step):
            columns = block_columns(step)
            more = jnp.dot(
                left, tokens_of(g, t, group, columns), preferred_element_type=jnp.float32
            )
            part[t, :, columns] = part[t, :, columns] + more if group else more

    before = none
    for segment, ends in enumerate(Z_ENDS):
        if ends != before:

            @pl.loop(pick(before), pick(ends))
            def _(e):
                z_event(e)

        before = ends
        if segment == len(Z_ENDS) - 1:
            break
        for stage, table in zip(stages, STAGE_ENDS):
            since = table[segment - 1] if segment else none
            if table[segment] != since:
                run(stage, since, table[segment])

    since_1, since_2, since_3, since_4 = (table[-1] for table in STAGE_ENDS)
    three, four = (3,) * sections, (4,) * sections
    run(stage_1, since_1, four)
    run(stage_2, since_2, three)
    add_up(0, 0)
    run(stage_2, three, four)
    run(stage_3, since_3, four)
    add_up(1, 0)

    run(stage_4, since_4, four, permuted=False)

    for t in range(2):
        for m in range(2):
            take(t, m, SIBLING + 1)
            whole(t, m, 0, 2 * PLANE - 1, SIBLING).wait_send()

        @pl.when(place(t) < sections - 1)
        def _():
            pltpu.make_async_remote_copy(
                src_ref=zbuf.at[t],
                dst_ref=zbuf.at[t],
                send_sem=zsend.at[t],
                recv_sem=zrecv.at[t, 0, 0],
                device_id=(lax.rem(s + 1 - 2 * t + sections, sections), j),
                device_id_type=pl.DeviceIdType.MESH,
            ).wait_send()


def gathered(deltas, backs, gains):
    _, micro, rows, width = deltas.shape
    return pl.pallas_call(
        gather_kernel,
        out_shape=(
            pltpu.VMEM((2, micro, 2 * PLANE, rows, width), jnp.bfloat16),
            pltpu.VMEM((2, width // lax.axis_size("shard"), width), jnp.float32),
        ),
        in_specs=[
            pl.BlockSpec(memory_space=pltpu.HBM),
            pl.BlockSpec(memory_space=pltpu.HBM),
            pl.BlockSpec(memory_space=pltpu.HBM),
        ],
        out_specs=(pl.BlockSpec(memory_space=pltpu.VMEM), pl.BlockSpec(memory_space=pltpu.VMEM)),
        scratch_shapes=[
            pltpu.VMEM((2, micro, rows, width), jnp.bfloat16),
            pltpu.VMEM((1, width), jnp.float32),
            pltpu.VMEM((2, micro, CHUNKS, rows, width // CHUNKS), jnp.float32),
            pltpu.VMEM((micro, rows, LANES), jnp.float32),
            pltpu.SemaphoreType.DMA((3,)),
            pltpu.SemaphoreType.DMA((2,)),
            pltpu.SemaphoreType.DMA((2, micro, CHUNKS)),
            pltpu.SemaphoreType.DMA((2, micro)),
            pltpu.SemaphoreType.DMA((2, micro, len(WAITS))),
        ],
        compiler_params=pltpu.CompilerParams(
            collective_id=0, has_side_effects=True, vmem_limit_bytes=20 * 2**20
        ),
        name="gather",
    )(*(pltpu.with_memory_space_constraint(a, pltpu.HBM) for a in (deltas, backs, gains)))


def covariance_kernel(g, part, act, grad, left, rows, sem):
    _, micro, slots, low, width = g.shape
    tokens = micro * slots * low
    tile = part.shape[1]
    last = len(GROUPS) - 1
    outs = (act, grad)
    for t in range(2):
        left[t] = tokens_of(g, t, last, own_columns(tile)).T
    writes = []
    for step in range(width // LAST_BLOCK):
        columns = pl.ds(step * LAST_BLOCK, LAST_BLOCK)
        for t in range(2):
            full = part[t, :, columns] + jnp.dot(
                left[t], tokens_of(g, t, last, columns), preferred_element_type=jnp.float32
            )
            rows[t, :, columns] = (full / tokens).astype(jnp.bfloat16)
            write = pltpu.make_async_copy(
                rows.at[t, :, columns], outs[t].at[0, :, columns], sem.at[t, step]
            )
            write.start()
            writes.append(write)
    for write in writes:
        write.wait()


def shards(deltas, backs, gains):
    width = deltas.shape[-1]
    tile = width // lax.axis_size("shard")
    g, part = gathered(deltas, backs, gains)
    _, micro, slots, low, _ = g.shape
    late_tokens = micro * low * (slots - GROUP_ENDS[-2])
    out = jax.ShapeDtypeStruct((1, tile, width), jnp.bfloat16)
    return pl.pallas_call(
        covariance_kernel,
        out_shape=(out, out),
        in_specs=[pl.BlockSpec(memory_space=pltpu.VMEM)] * 2,
        out_specs=(pl.BlockSpec(memory_space=pl.ANY), pl.BlockSpec(memory_space=pl.ANY)),
        scratch_shapes=[
            pltpu.VMEM((2, tile, late_tokens), jnp.bfloat16),
            pltpu.VMEM((2, tile, width), jnp.bfloat16),
            pltpu.SemaphoreType.DMA((2, width // LAST_BLOCK)),
        ],
        compiler_params=pltpu.CompilerParams(vmem_limit_bytes=20 * 2**20),
        name="covariance",
    )(*(pltpu.with_memory_space_constraint(a, pltpu.VMEM) for a in (g, part)))


def solution(mesh):
    return jax.shard_map(
        shards,
        mesh=mesh,
        in_specs=(
            P("section", None, "shard", None),
            P("section", None, "shard", None),
            P("section", None),
        ),
        out_specs=(P("section", "shard", None), P("section", "shard", None)),
        check_vma=False,
    )
```
